128 devices in a mesh: ta: 4 (over y), gx: 32 (over x, z, core).
Axes of the slice: x: 4, y: 4, z: 4, core: 2. Of those that a mesh axis runs over, the one named last changes fastest.
Arguments:
- eigvecs: bfloat16 [4, 16384, 3, 2, 384], P('ta', 'gx'), may hold values from -0.01953125 to 0.01953125
- perambulators: bfloat16 [4, 2, 384, 4, 4, 384], P('ta', None, 'gx'), may hold values from -0.59765625 to 0.59765625
- source_blocks: bfloat16 [9, 2, 384, 384], replicated, may hold values from -0.3125 to 0.3125
- momenta: int32 [9, 3], replicated, may hold values from -2 to 2
- op_momentum: int32 [64], replicated, may hold values from 0 to 8
- op_gamma: int32 [64], replicated, may hold values from 0 to 15
- ref_vectors: float32 [2, 64, 8], replicated, may hold values from -0.75 to 0.75
Outputs:
- correlator: float32 [4, 2, 64, 64], P('ta')
- projected: float32 [4, 2, 8, 8], P('ta')
The draws below stay inside these ranges and needn't reach their ends.
All inputs are finite; a program needn't handle non-finite values.
Results may differ from the reference program's by a relative error of at most 0.0055.
Values may be sent and summed in bfloat16 or wider, within the bound.
No kernel may reach another device: no remote copies, remote signals or barrier semaphores. Data moves between devices by JAX's collectives and lax.ppermute only.
A program may use at most 128 MiB of HBM per device.

```python
import math
import jax
import jax.numpy as jnp
import numpy as np
from jax import lax

EXTENT = 96
NEV = 384
NMOM = 9
NOPS = 64
NVEC = 8
TIMES = 4
SPACE = 16384


def set_ends(result, key, least, largest):
    spot = [jax.random.randint(jax.random.fold_in(key, axis), (), 0, length) for axis, length in enumerate(result.shape)]
    widest = result.shape.index(max(result.shape))
    neighbour = spot[:widest] + [(spot[widest] + 1) % result.shape[widest]] + spot[widest + 1:]
    return result.at[tuple(spot)].set(least).at[tuple(neighbour)].set(largest)


def levels(stream_key, extent, split, smallest, top_value):
    level = 1.0
    for dim, parts in split:
        steps = jax.random.uniform(jax.random.fold_in(jax.random.fold_in(stream_key, 6), dim), (parts,), jnp.float32, smallest / len(split), top_value / len(split))
        level = level * jnp.repeat(jnp.exp(steps), extent[dim] // parts).reshape((-1,) + (1,) * (len(extent) - 1 - dim))
    return level


def bell_draw(key, extent, width, reach, split=(), held_as=jnp.bfloat16):
    entries = width * jax.random.normal(key, extent, jnp.float32)
    if split:
        entries = entries * levels(key, extent, split, -0.22, 0.18)
    return jnp.clip(entries, -reach, reach).astype(held_as)


def setup_inputs(seed: int = 0) -> dict:
    arg_keys = jax.random.split(jax.random.key(seed), 8)
    eigvecs = bell_draw(arg_keys[0], (TIMES, SPACE, 3, 2, NEV), (6 * SPACE) ** -0.5, 0.01953125, ((0, 4), (1, 32)))
    perambulators = bell_draw(arg_keys[1], (TIMES, 2, NEV, 4, 4, NEV), 0.1, 0.59765625, ((0, 4), (2, 32)))
    source_blocks = bell_draw(arg_keys[2], (NMOM, 2, NEV, NEV), NEV ** -0.5, 0.3125)
    momenta = set_ends(jax.random.randint(arg_keys[3], (NMOM, 3), -2, 3), jax.random.fold_in(arg_keys[3], 1), -2, 2).astype(jnp.int32)
    op_momentum = set_ends(jax.random.randint(arg_keys[4], (NOPS,), 0, NMOM), jax.random.fold_in(arg_keys[4], 1), 0, NMOM - 1).astype(jnp.int32)
    op_gamma = set_ends(jax.random.randint(arg_keys[5], (NOPS,), 0, 16), jax.random.fold_in(arg_keys[5], 1), 0, 15).astype(jnp.int32)
    ref_vectors = bell_draw(arg_keys[6], (2, NOPS, NVEC), NOPS ** -0.5, 0.75, (), jnp.float32)
    return dict(eigvecs=eigvecs, perambulators=perambulators, source_blocks=source_blocks, momenta=momenta, op_momentum=op_momentum, op_gamma=op_gamma, ref_vectors=ref_vectors)


full_precision = lax.Precision.HIGHEST

def gamma_tables():
    zero_block = np.zeros((4, 4), np.float32)
    first_imag = np.array([[0, 0, 0, 1], [0, 0, 1, 0], [0, -1, 0, 0], [-1, 0, 0, 0]], np.float32)
    second_real = np.array([[0, 0, 0, -1], [0, 0, 1, 0], [0, 1, 0, 0], [-1, 0, 0, 0]], np.float32)
    third_imag = np.array([[0, 0, 1, 0], [0, 0, 0, -1], [-1, 0, 0, 0], [0, 1, 0, 0]], np.float32)
    fourth_real = np.array([[0, 0, 1, 0], [0, 0, 0, 1], [1, 0, 0, 0], [0, 1, 0, 0]], np.float32)
    gamma_list = [(zero_block, first_imag), (second_real, zero_block), (zero_block, third_imag), (fourth_real, zero_block)]
    real_parts = []
    imag_parts = []
    for subset in range(16):
        prod_real = np.eye(4, dtype=np.float32)
        prod_imag = np.zeros((4, 4), np.float32)
        for position in range(4):
            if subset >> position & 1:
                factor_real, factor_imag = gamma_list[position]
                prod_real, prod_imag = (prod_real @ factor_real - prod_imag @ factor_imag, prod_real @ factor_imag + prod_imag @ factor_real)
        real_parts.append(prod_real)
        imag_parts.append(prod_imag)
    return (np.stack(real_parts).astype(np.float32), np.stack(imag_parts).astype(np.float32))

def complex_einsum(form, left_real, left_imag, right_real, right_imag):

    def single(left_part, right_part):
        return jnp.einsum(form, left_part, right_part, precision=full_precision, preferred_element_type=jnp.float32)
    return (single(left_real, right_real) - single(left_imag, right_imag), single(left_real, right_imag) + single(left_imag, right_real))

def phase_factors(momenta, site_ids):
    xcoord = site_ids % EXTENT
    ycoord = site_ids // EXTENT % EXTENT
    zcoord = site_ids // (EXTENT * EXTENT)
    winding = (momenta[:, 0:1] * xcoord[None, :] + momenta[:, 1:2] * ycoord[None, :] + momenta[:, 2:3] * zcoord[None, :]) % EXTENT
    phase_angle = winding.astype(jnp.float32) * (-2.0 * math.pi / EXTENT)
    return (jnp.cos(phase_angle), jnp.sin(phase_angle))

def right_block(vec_real, vec_imag, cosine, sine_row):
    cosine = cosine[:, None, None]
    sine_row = sine_row[:, None, None]
    eig_width = vec_real.shape[-1]
    twist_real = (cosine * vec_real - sine_row * vec_imag).astype(jnp.bfloat16).reshape(-1, eig_width)
    twist_imag = (cosine * vec_imag + sine_row * vec_real).astype(jnp.bfloat16).reshape(-1, eig_width)
    upper = jnp.concatenate([twist_real, twist_imag], 1)
    lower = jnp.concatenate([twist_imag, -twist_real], 1)
    return jnp.concatenate([upper, lower], 0)

def assemble(blocks_real, blocks_imag, op_momentum, op_gamma):
    table_real, table_imag = gamma_tables()
    chosen = (op_gamma[:, None] == jnp.arange(16, dtype=jnp.int32)[None, :]).astype(jnp.float32)
    gre = jnp.einsum('ig,gax->iax', chosen, jnp.asarray(table_real), precision=full_precision)
    gim = jnp.einsum('ig,gax->iax', chosen, jnp.asarray(table_imag), precision=full_precision)
    moment = (op_momentum[:, None] == jnp.arange(NMOM, dtype=jnp.int32)[None, :]).astype(jnp.float32)
    chiral = jnp.asarray(np.array([1.0, 1.0, -1.0, -1.0], np.float32))
    weight_left = moment[:, :, None, None] * chiral[None, None, None, :]
    left_real = weight_left * jnp.transpose(gre, (0, 2, 1))[:, None]
    left_imag = weight_left * jnp.transpose(gim, (0, 2, 1))[:, None]
    lifted_real, lifted_imag = complex_einsum('imxa,mxynwa->iynw', left_real, left_imag, blocks_real, blocks_imag)
    weight_right = moment[:, :, None, None] * chiral[None, None, None, :]
    right_real = weight_right * jnp.transpose(gre, (0, 2, 1))[:, None]
    right_imag = -weight_right * jnp.transpose(gim, (0, 2, 1))[:, None]
    return complex_einsum('iynw,jnyw->ij', lifted_real, lifted_imag, right_real, right_imag)

def project(corr_real, corr_imag, ref_vectors):
    basis_real = ref_vectors[0]
    basis_imag = ref_vectors[1]
    half_real, half_imag = complex_einsum('ij,jv->iv', corr_real, corr_imag, basis_real, basis_imag)
    return complex_einsum('iu,iv->uv', basis_real, -basis_imag, half_real, half_imag)

def reference(eigvecs, perambulators, source_blocks, momenta, op_momentum, op_gamma, ref_vectors):
    site_ids = jnp.arange(SPACE, dtype=jnp.int32)
    cosine, sine_row = phase_factors(momenta, site_ids)
    correlators = []
    raw_list = []
    for slice_index in range(TIMES):
        vectors = eigvecs[slice_index]
        vec_real = vectors[:, :, 0, :]
        vec_imag = vectors[:, :, 1, :]
        conj_left = jnp.concatenate([vec_real.reshape(-1, NEV), vec_imag.reshape(-1, NEV)], 0).astype(jnp.float32)
        pieces = []
        for moment_index in range(NMOM):
            twist_right = right_block(vec_real, vec_imag, cosine[moment_index], sine_row[moment_index]).astype(jnp.float32)
            summed = lax.dot_general(conj_left, twist_right, (((0,), (0,)), ((), ())), precision=full_precision, preferred_element_type=jnp.float32)
            pieces.append(summed.reshape(NEV, 2, NEV))
        phase_rows = jnp.stack(pieces, 1).astype(jnp.bfloat16).astype(jnp.float32)
        peram = perambulators[slice_index].astype(jnp.float32)
        sink_real, sink_imag = complex_einsum('rml,labk->mrabk', phase_rows[:, :, 0], phase_rows[:, :, 1], peram[0], peram[1])
        sink_real = sink_real.astype(jnp.bfloat16).astype(jnp.float32)
        sink_imag = sink_imag.astype(jnp.bfloat16).astype(jnp.float32)
        source = source_blocks.astype(jnp.float32)
        src_real, src_imag = complex_einsum('rabl,nkl->rabnk', peram[0], -peram[1], source[:, 0], source[:, 1])
        src_real = src_real.astype(jnp.bfloat16).astype(jnp.float32)
        src_imag = src_imag.astype(jnp.bfloat16).astype(jnp.float32)
        blocks_real, blocks_imag = complex_einsum('mrxyk,rawnk->mxynwa', sink_real, sink_imag, src_real, src_imag)
        corr_real, corr_imag = assemble(blocks_real, blocks_imag, op_momentum, op_gamma)
        correlators.append(jnp.stack([corr_real, corr_imag]))
        proj_real, proj_imag = project(corr_real, corr_imag, ref_vectors)
        raw_list.append(jnp.stack([proj_real, proj_imag]))
    first = raw_list[0]
    mean_square = jnp.mean(first * first)
    scale_factor = lax.rsqrt(mean_square + 1e-06)
    return (jnp.stack(correlators), jnp.stack(raw_list) * scale_factor)
```

```python
import functools
import math

import jax
import jax.numpy as jnp
import numpy as np
from jax import lax
from jax.experimental import pallas as pl
from jax.experimental.pallas import tpu as pltpu
from jax.sharding import PartitionSpec as P

EXTENT = 96
NMOM = 9
BF = jnp.bfloat16
F32 = jnp.float32
HALF_PERIOD = -2.0 * math.pi / EXTENT
CHUNK = 768
ROWS = 24
MPAD = 16
VMEM = 60 << 20
full_precision = lax.Precision.HIGHEST
SAME_CORE = [[d for d in range(32) if d % 2 == c] for c in range(2)]
PAIR = [(d, d ^ 1) for d in range(32)]


def gamma_tables():
    zero_block = np.zeros((4, 4), np.float32)
    first_imag = np.array([[0, 0, 0, 1], [0, 0, 1, 0], [0, -1, 0, 0], [-1, 0, 0, 0]], np.float32)
    second_real = np.array([[0, 0, 0, -1], [0, 0, 1, 0], [0, 1, 0, 0], [-1, 0, 0, 0]], np.float32)
    third_imag = np.array([[0, 0, 1, 0], [0, 0, 0, -1], [-1, 0, 0, 0], [0, 1, 0, 0]], np.float32)
    fourth_real = np.array([[0, 0, 1, 0], [0, 0, 0, 1], [1, 0, 0, 0], [0, 1, 0, 0]], np.float32)
    gamma_list = [
        (zero_block, first_imag),
        (second_real, zero_block),
        (zero_block, third_imag),
        (fourth_real, zero_block),
    ]
    real_parts = []
    imag_parts = []
    for subset in range(16):
        prod_real = np.eye(4, dtype=np.float32)
        prod_imag = np.zeros((4, 4), np.float32)
        for position in range(4):
            if subset >> position & 1:
                factor_real, factor_imag = gamma_list[position]
                prod_real, prod_imag = (
                    prod_real @ factor_real - prod_imag @ factor_imag,
                    prod_real @ factor_imag + prod_imag @ factor_real,
                )
        real_parts.append(prod_real)
        imag_parts.append(prod_imag)
    return (np.stack(real_parts).astype(np.float32), np.stack(imag_parts).astype(np.float32))


def spin_tables():
    chiral = np.array([1.0, 1.0, -1.0, -1.0], np.float32)
    parts = np.stack(gamma_tables())
    left = np.transpose(parts, (0, 2, 1, 3)) * chiral[None, :, None, None]
    left = np.repeat(left[..., None], MPAD, -1).reshape(2, 4, 16, 4 * MPAD)
    right = np.transpose(parts, (0, 3, 1, 2)) * chiral
    right = right * np.array([1.0, -1.0], np.float32)[:, None, None, None]
    right = np.broadcast_to(right[:, :, :, None, None, :], (2, 4, 16, NMOM, 4, 4))
    return left, right.reshape(2, 4, 16, NMOM * 16)


def dot(left, right, lc, rc, precision=None):
    return lax.dot_general(
        left, right, (((lc,), (rc,)), ((), ())), precision=precision, preferred_element_type=F32
    )


def phase_kernel(first, full, half, steps, where_ref, mom_ref, own_ref, other_ref, out_ref, acc_ref):
    step = pl.program_id(0)
    core = lax.rem(where_ref[0], 2)
    is_own = step < steps
    real = jnp.where(is_own, own_ref[0], other_ref[0])
    imag = jnp.where(is_own, own_ref[1], other_ref[1])
    left = jnp.concatenate([real.T, imag.T], 1)
    device = jnp.where(is_own, where_ref[0], where_ref[0] + 1 - 2 * core)
    unit = lax.broadcasted_iota(jnp.int32, (8, CHUNK), 0)
    row = lax.rem(step, steps) * CHUNK + lax.broadcasted_iota(jnp.int32, (8, CHUNK), 1)
    site = jnp.floor((row.astype(F32) + 0.5) * (1.0 / 3.0)) + (device * 512).astype(F32)
    line = jnp.floor((site + 0.5) * (1.0 / EXTENT))
    xcoord = site - EXTENT * line
    zcoord = jnp.floor((line + 0.5) * (1.0 / EXTENT))
    ycoord = line - EXTENT * zcoord
    winding = jnp.zeros((8, CHUNK), F32)
    for u in range(full + half):
        m = 4 * core + first + u if u < full else NMOM - 1
        here = (
            mom_ref[3 * m].astype(F32) * xcoord
            + mom_ref[3 * m + 1].astype(F32) * ycoord
            + mom_ref[3 * m + 2].astype(F32) * zcoord
        )
        winding = jnp.where(unit == u, here, winding)
    winding = winding - EXTENT * jnp.floor((winding + 0.5) * (1.0 / EXTENT))
    angle = winding * HALF_PERIOD
    cosine = jnp.cos(angle)
    sine = jnp.sin(angle)
    if half:
        turned = jnp.logical_and(unit == full, core == 1)
        cosine, sine = jnp.where(turned, sine, cosine), jnp.where(turned, -cosine, sine)
    cosine = cosine.T
    sine = sine.T
    real = real.astype(F32)
    imag = imag.astype(F32)

    @pl.when(step == 0)
    def _():
        acc_ref[...] = jnp.zeros_like(acc_ref)

    for u in range(full + half):
        c = cosine[:, u : u + 1]
        s = sine[:, u : u + 1]
        twist_real = (c * real - s * imag).astype(BF)
        twist_imag = (c * imag + s * real).astype(BF)
        if u < full:
            right = jnp.concatenate(
                [
                    jnp.concatenate([twist_real, twist_imag], 1),
                    jnp.concatenate([twist_imag, -twist_real], 1),
                ],
                0,
            )
        else:
            right = jnp.concatenate([twist_real, twist_imag], 0)
        at = slice(768 * u, 768 * u + right.shape[1])
        acc_ref[:, at] += dot(left, right, 1, 0)

    @pl.when(step == 2 * steps - 1)
    def _():
        for j in range(16):
            out_ref[j] = acc_ref[ROWS * j : ROWS * (j + 1), :].astype(BF)


def phase_part(own, other, where, momenta, first, full, half):
    steps = own.shape[1] // CHUNK
    width = 768 * full + 384 * half
    return pl.pallas_call(
        functools.partial(phase_kernel, first, full, half, steps),
        grid_spec=pltpu.PrefetchScalarGridSpec(
            num_scalar_prefetch=2,
            grid=(2 * steps,),
            in_specs=[
                pl.BlockSpec((2, CHUNK, 384), lambda c, *_: (0, jnp.minimum(c, steps - 1), 0)),
                pl.BlockSpec((2, CHUNK, 384), lambda c, *_: (0, jnp.maximum(c - steps, 0), 0)),
            ],
            out_specs=pl.BlockSpec((16, ROWS, width), lambda c, *_: (0, 0, 0)),
            scratch_shapes=[pltpu.VMEM((384, width), F32)],
        ),
        out_shape=jax.ShapeDtypeStruct((16, ROWS, width), BF),
        compiler_params=pltpu.CompilerParams(vmem_limit_bytes=VMEM),
        name=f"phase_{first}",
    )(where, momenta, own, other)


def source_kernel(
    where_ref, tau_ref, src_ref, mom_ref, gam_ref, ltab_ref, rtab_ref, out_ref, left_ref, right_ref
):
    n = pl.program_id(0)
    x = jnp.concatenate([tau_ref[:, 0].reshape(384, 384), tau_ref[:, 1].reshape(384, 384)], 1)
    s_real = src_ref[0, 0]
    s_imag = src_ref[0, 1]
    to_real = jnp.concatenate([s_real, s_imag], 1)
    to_imag = jnp.concatenate([s_imag, -s_real], 1)
    out_ref[:, 0, 0] = dot(x, to_real, 1, 1).astype(BF).reshape(ROWS, 16, 192)
    out_ref[:, 1, 0] = dot(x, to_imag, 1, 1).astype(BF).reshape(ROWS, 16, 192)

    @pl.when(n == 0)
    def _():
        chosen = (gam_ref[...] == lax.broadcasted_iota(jnp.int32, (64, 16), 1)).astype(BF)
        lane = lax.rem(lax.broadcasted_iota(jnp.int32, (64, 64), 1), MPAD)
        moment = mom_ref[...] == lane
        for a in range(4):
            for q in range(2):
                got = jnp.where(moment, dot(chosen, ltab_ref[q, a], 1, 0), 0.0)
                left_ref[q, 64 * a : 64 * a + 64, :] = got
        lane = lax.broadcasted_iota(jnp.int32, (64, 144), 1)
        low = mom_ref[...] * 16
        moment = jnp.logical_and(lane >= low, lane < low + 16)
        for y in range(4):
            for q in range(2):
                right_ref[q, y] = jnp.where(moment, dot(chosen, rtab_ref[q, y], 1, 0), 0.0)


def source_part(tau, source_blocks, op_momentum, op_gamma, where):
    ltab, rtab = spin_tables()
    whole = lambda shape: pl.BlockSpec(shape, lambda n, *_: (0,) * len(shape))
    return pl.pallas_call(
        source_kernel,
        grid_spec=pltpu.PrefetchScalarGridSpec(
            num_scalar_prefetch=1,
            grid=(NMOM,),
            in_specs=[
                whole((ROWS, 2, 16, 384)),
                pl.BlockSpec((1, 2, 192, 384), lambda n, w: (n, 0, lax.rem(w[0], 2), 0)),
                whole((64, 1)),
                whole((64, 1)),
                whole((2, 4, 16, 64)),
                whole((2, 4, 16, 144)),
            ],
            out_specs=[
                pl.BlockSpec((ROWS, 2, 1, 16, 192), lambda n, *_: (0, 0, n, 0, 0)),
                whole((2, 256, 64)),
                whole((2, 4, 64, 144)),
            ],
        ),
        out_shape=[
            jax.ShapeDtypeStruct((ROWS, 2, NMOM, 16, 192), BF),
            jax.ShapeDtypeStruct((2, 256, 64), F32),
            jax.ShapeDtypeStruct((2, 4, 64, 144), F32),
        ],
        compiler_params=pltpu.CompilerParams(vmem_limit_bytes=VMEM),
        name="source",
    )(
        where,
        tau,
        source_blocks,
        op_momentum[:, None],
        op_gamma[:, None],
        jnp.asarray(ltab, BF),
        jnp.asarray(rtab, BF),
    )


def sink_kernel(
    where_ref, own1, oth1, own2, oth2, tau_ref, src_ref, left_ref, right_ref, out_ref,
    rows_ref, sink_ref, acc_ref,
):
    core = lax.rem(where_ref[0], 2)
    rows_ref[...] = jnp.zeros_like(rows_ref)
    for c in range(2):
        one = jnp.where(core == c, own1[...], oth1[...]).astype(F32)
        two = jnp.where(core == c, own2[...], oth2[...]).astype(F32)
        for u in range(4):
            part = one if u < 2 else two
            for q in range(2):
                at = 768 * (u % 2) + 384 * q
                rows_ref[q, :, 4 * c + u, :] = part[:, at : at + 384]
        rows_ref[c, :, 8, :] = two[:, 1536:1920]
    real = rows_ref[0].reshape(384, 384).astype(BF)
    imag = rows_ref[1].reshape(384, 384).astype(BF)
    stacked = jnp.concatenate(
        [jnp.concatenate([real, -imag], 1), jnp.concatenate([imag, real], 1)], 0
    )
    for g in range(4):
        at = slice(768 * g, 768 * g + 768)
        here = jnp.concatenate([tau_ref[:, at], tau_ref[:, 3072 + 768 * g : 3840 + 768 * g]], 0)
        got = dot(stacked, here, 1, 0).astype(BF)
        for y in range(4):
            for q in range(2):
                sink_ref[q, 4 * y + g] = got[384 * q : 384 * q + 384, 192 * y : 192 * y + 192]
    acc_ref[...] = jnp.zeros_like(acc_ref)

    def one_row(r, carry):
        at = pl.ds(pl.multiple_of(r * MPAD, MPAD), MPAD)
        left = jnp.concatenate([sink_ref[q, :, at, :].reshape(256, 192) for q in range(2)], 0)
        right = src_ref[r].reshape(288, 192)
        acc_ref[...] += dot(left, right, 1, 1)
        return carry

    lax.fori_loop(0, ROWS, one_row, 0)
    acc = acc_ref[...]
    block_real = acc[:256, :144] - acc[256:, 144:]
    block_imag = acc[:256, 144:] + acc[256:, :144]
    l_real = left_ref[0]
    l_imag = left_ref[1]
    lifted = jnp.concatenate(
        [jnp.concatenate([l_real, -l_imag], 1), jnp.concatenate([l_imag, l_real], 1)], 0
    )
    spin = lax.rem(lax.broadcasted_iota(jnp.int32, (64, 144), 1), 16) // 4
    corr_real = jnp.zeros((64, 64), F32)
    corr_imag = jnp.zeros((64, 64), F32)
    for y in range(4):
        at = slice(64 * y, 64 * y + 64)
        both = jnp.concatenate([block_real[at], block_imag[at]], 0)
        got = dot(lifted, both, 1, 0, full_precision)
        halves = []
        for q in range(2):
            total = jnp.zeros((64, 144), F32)
            for a in range(4):
                low = 256 * q + 64 * a
                total = jnp.where(spin == a, got[low : low + 64], total)
            halves.append(total)
        r_real = right_ref[0, y]
        r_imag = right_ref[1, y]
        corr_real += dot(halves[0], r_real, 1, 1, full_precision)
        corr_real -= dot(halves[1], r_imag, 1, 1, full_precision)
        corr_imag += dot(halves[0], r_imag, 1, 1, full_precision)
        corr_imag += dot(halves[1], r_real, 1, 1, full_precision)
    out_ref[0] = corr_real
    out_ref[1] = corr_imag


def sink_part(where, own1, oth1, own2, oth2, tau, src, left, right):
    specs = [pl.BlockSpec(memory_space=pltpu.VMEM)] * 8
    return pl.pallas_call(
        sink_kernel,
        grid_spec=pltpu.PrefetchScalarGridSpec(
            num_scalar_prefetch=1,
            grid=(),
            in_specs=specs,
            out_specs=pl.BlockSpec(memory_space=pltpu.VMEM),
            scratch_shapes=[
                pltpu.VMEM((2, ROWS, MPAD, 384), F32),
                pltpu.VMEM((2, 16, 384, 192), BF),
                pltpu.VMEM((512, 288), F32),
            ],
        ),
        out_shape=jax.ShapeDtypeStruct((2, 64, 64), F32),
        compiler_params=pltpu.CompilerParams(vmem_limit_bytes=VMEM),
        name="sink",
    )(where, own1, oth1, own2, oth2, tau, src, left, right)


def complex_einsum(form, left_real, left_imag, right_real, right_imag):

    def single(left_part, right_part):
        return jnp.einsum(
            form,
            left_part,
            right_part,
            precision=full_precision,
            preferred_element_type=jnp.float32,
        )

    return (
        single(left_real, right_real) - single(left_imag, right_imag),
        single(left_real, right_imag) + single(left_imag, right_real),
    )


def project(corr_real, corr_imag, ref_vectors):
    basis_real = ref_vectors[0]
    basis_imag = ref_vectors[1]
    half_real, half_imag = complex_einsum("ij,jv->iv", corr_real, corr_imag, basis_real, basis_imag)
    return complex_einsum("iu,iv->uv", basis_real, -basis_imag, half_real, half_imag)


def taken_together(shard, axis):
    length = lax.axis_size(axis)
    spread = jnp.broadcast_to(shard[None], (length, *shard.shape))
    return jnp.sum(lax.all_to_all(spread, axis, 0, 0, tiled=True), axis=0)


def picked(shard, axis, root):
    return lax.dynamic_index_in_dim(lax.all_gather(shard, axis), root, 0, keepdims=False)


def scattered(part):
    got = lax.all_to_all(part, "gx", 0, 0, tiled=True, axis_index_groups=SAME_CORE)
    return jnp.sum(got.astype(F32), 0).astype(BF)


def body(eigvecs, perambulators, source_blocks, momenta, op_momentum, op_gamma, ref_vectors):
    device = lax.axis_index("gx")
    core = device % 2
    where = device[None]
    own = jnp.transpose(eigvecs.reshape(-1, 2, 384), (1, 0, 2))
    other = lax.ppermute(own, "gx", PAIR)
    mine = jnp.transpose(perambulators[0], (1, 0, 2, 3, 4)).reshape(12, 2, 16, 384)
    theirs = lax.ppermute(mine, "gx", PAIR)
    tau = jnp.where(
        core == 0, jnp.concatenate([mine, theirs], 0), jnp.concatenate([theirs, mine], 0)
    )
    part = jnp.where(core == 0, tau[..., :192], tau[..., 192:]).reshape(ROWS, 6144)
    tau_all = lax.all_gather(part, "gx", axis=0, tiled=True, axis_index_groups=SAME_CORE)
    flat = momenta.reshape(-1)
    first = phase_part(own, other, where, flat, 0, 2, 0)
    own1 = scattered(first)
    second = phase_part(own, other, where, flat, 2, 2, 1)
    own2 = scattered(second)
    oth1 = lax.ppermute(own1, "gx", PAIR)
    oth2 = lax.ppermute(own2, "gx", PAIR)
    src, left, right = source_part(tau, source_blocks, op_momentum, op_gamma, where)
    corr = sink_part(where, own1, oth1, own2, oth2, tau_all, src, left, right)
    corr = taken_together(corr.reshape(-1), "gx").reshape(2, 64, 64)
    proj_real, proj_imag = project(corr[0], corr[1], ref_vectors)
    raw_pair = jnp.stack([proj_real, proj_imag])
    local_square = jnp.mean(raw_pair * raw_pair)
    first_square = picked(local_square, "ta", 0)
    scale_factor = lax.rsqrt(first_square + 1e-06)
    return (corr[None], (raw_pair * scale_factor)[None])


def solution(mesh):
    placed = (
        P("ta", "gx", None, None, None),
        P("ta", None, "gx", None, None, None),
        P(),
        P(),
        P(),
        P(),
        P(),
    )
    return jax.shard_map(
        body,
        mesh=mesh,
        in_specs=placed,
        out_specs=(P("ta", None, None, None), P("ta", None, None, None)),
        check_vma=False,
    )
```

```python
import functools
import math

import jax
import jax.numpy as jnp
import numpy as np
from jax import lax
from jax.experimental import pallas as pl
from jax.experimental.pallas import tpu as pltpu
from jax.sharding import PartitionSpec as P

EXTENT = 96
NMOM = 9
BF = jnp.bfloat16
F32 = jnp.float32
HALF_PERIOD = -2.0 * math.pi / EXTENT
CHUNK = 768
ROWS = 24
MPAD = 16
VMEM = 60 << 20
full_precision = lax.Precision.HIGHEST
SAME_CORE = [[d for d in range(32) if d % 2 == c] for c in range(2)]
PAIR = [(d, d ^ 1) for d in range(32)]


def shift(x, z):
    ring = [(i, j, c) for i in range(4) for j in range(4) for c in range(2)]
    number = lambda i, j, c: i % 4 * 8 + j % 4 * 2 + c
    return [(number(i, j, c), number(i + x, j + z, c)) for i, j, c in ring]


def gamma_tables():
    zero_block = np.zeros((4, 4), np.float32)
    first_imag = np.array([[0, 0, 0, 1], [0, 0, 1, 0], [0, -1, 0, 0], [-1, 0, 0, 0]], np.float32)
    second_real = np.array([[0, 0, 0, -1], [0, 0, 1, 0], [0, 1, 0, 0], [-1, 0, 0, 0]], np.float32)
    third_imag = np.array([[0, 0, 1, 0], [0, 0, 0, -1], [-1, 0, 0, 0], [0, 1, 0, 0]], np.float32)
    fourth_real = np.array([[0, 0, 1, 0], [0, 0, 0, 1], [1, 0, 0, 0], [0, 1, 0, 0]], np.float32)
    gamma_list = [
        (zero_block, first_imag),
        (second_real, zero_block),
        (zero_block, third_imag),
        (fourth_real, zero_block),
    ]
    real_parts = []
    imag_parts = []
    for subset in range(16):
        prod_real = np.eye(4, dtype=np.float32)
        prod_imag = np.zeros((4, 4), np.float32)
        for position in range(4):
            if subset >> position & 1:
                factor_real, factor_imag = gamma_list[position]
                prod_real, prod_imag = (
                    prod_real @ factor_real - prod_imag @ factor_imag,
                    prod_real @ factor_imag + prod_imag @ factor_real,
                )
        real_parts.append(prod_real)
        imag_parts.append(prod_imag)
    return (np.stack(real_parts).astype(np.float32), np.stack(imag_parts).astype(np.float32))


def spin_tables():
    chiral = np.array([1.0, 1.0, -1.0, -1.0], np.float32)
    parts = np.stack(gamma_tables())
    left = np.transpose(parts, (0, 2, 1, 3)) * chiral[None, :, None, None]
    left = np.repeat(left[..., None], MPAD, -1).reshape(2, 4, 16, 4 * MPAD)
    right = np.transpose(parts, (0, 3, 1, 2)) * chiral
    right = right * np.array([1.0, -1.0], np.float32)[:, None, None, None]
    right = np.broadcast_to(right[:, :, :, None, None, :], (2, 4, 16, NMOM, 4, 4))
    return left, right.reshape(2, 4, 16, NMOM * 16)


def dot(left, right, lc, rc, precision=None):
    return lax.dot_general(
        left, right, (((lc,), (rc,)), ((), ())), precision=precision, preferred_element_type=F32
    )


def phase_kernel(first, full, half, steps, where_ref, mom_ref, own_ref, other_ref, out_ref, acc_ref):
    step = pl.program_id(0)
    core = lax.rem(where_ref[0], 2)
    is_own = step < steps
    real = jnp.where(is_own, own_ref[0], other_ref[0])
    imag = jnp.where(is_own, own_ref[1], other_ref[1])
    left = jnp.concatenate([real.T, imag.T], 1)
    device = jnp.where(is_own, where_ref[0], where_ref[0] + 1 - 2 * core)
    unit = lax.broadcasted_iota(jnp.int32, (8, CHUNK), 0)
    row = lax.rem(step, steps) * CHUNK + lax.broadcasted_iota(jnp.int32, (8, CHUNK), 1)
    site = jnp.floor((row.astype(F32) + 0.5) * (1.0 / 3.0)) + (device * 512).astype(F32)
    line = jnp.floor((site + 0.5) * (1.0 / EXTENT))
    xcoord = site - EXTENT * line
    zcoord = jnp.floor((line + 0.5) * (1.0 / EXTENT))
    ycoord = line - EXTENT * zcoord
    winding = jnp.zeros((8, CHUNK), F32)
    for u in range(full + half):
        m = 4 * core + first + u if u < full else NMOM - 1
        here = (
            mom_ref[3 * m].astype(F32) * xcoord
            + mom_ref[3 * m + 1].astype(F32) * ycoord
            + mom_ref[3 * m + 2].astype(F32) * zcoord
        )
        winding = jnp.where(unit == u, here, winding)
    winding = winding - EXTENT * jnp.floor((winding + 0.5) * (1.0 / EXTENT))
    angle = winding * HALF_PERIOD
    cosine = jnp.cos(angle)
    sine = jnp.sin(angle)
    if half:
        turned = jnp.logical_and(unit == full, core == 1)
        cosine, sine = jnp.where(turned, sine, cosine), jnp.where(turned, -cosine, sine)
    cosine = cosine.T
    sine = sine.T
    real = real.astype(F32)
    imag = imag.astype(F32)

    @pl.when(step == 0)
    def _():
        acc_ref[...] = jnp.zeros_like(acc_ref)

    for u in range(full + half):
        c = cosine[:, u : u + 1]
        s = sine[:, u : u + 1]
        twist_real = (c * real - s * imag).astype(BF)
        twist_imag = (c * imag + s * real).astype(BF)
        if u < full:
            right = jnp.concatenate(
                [
                    jnp.concatenate([twist_real, twist_imag], 1),
                    jnp.concatenate([twist_imag, -twist_real], 1),
                ],
                0,
            )
        else:
            right = jnp.concatenate([twist_real, twist_imag], 0)
        at = slice(768 * u, 768 * u + right.shape[1])
        acc_ref[:, at] += dot(left, right, 1, 0)

    @pl.when(step == 2 * steps - 1)
    def _():
        width = acc_ref.shape[1]
        diagonal = lax.broadcasted_iota(jnp.int32, (384, 384), 0) == lax.broadcasted_iota(
            jnp.int32, (384, 384), 1
        )
        lane = lax.broadcasted_iota(jnp.int32, (384, 128), 1)
        rest = jnp.zeros((384, 128), F32)
        for b in range(width // 384):
            block = acc_ref[:, 384 * b : 384 * b + 384]
            lost = jnp.where(diagonal, block - block.astype(BF).astype(F32), 0.0)
            rest = jnp.where(lane == b, jnp.sum(lost, 1, keepdims=True), rest)
        for j in range(16):
            at = slice(ROWS * j, ROWS * (j + 1))
            out_ref[j, :, :width] = acc_ref[at, :].astype(BF)
            out_ref[j, :, width:] = rest[at].astype(BF)


def phase_part(own, other, where, momenta, first, full, half):
    steps = own.shape[1] // CHUNK
    width = 768 * full + 384 * half
    return pl.pallas_call(
        functools.partial(phase_kernel, first, full, half, steps),
        grid_spec=pltpu.PrefetchScalarGridSpec(
            num_scalar_prefetch=2,
            grid=(2 * steps,),
            in_specs=[
                pl.BlockSpec((2, CHUNK, 384), lambda c, *_: (0, jnp.minimum(c, steps - 1), 0)),
                pl.BlockSpec((2, CHUNK, 384), lambda c, *_: (0, jnp.maximum(c - steps, 0), 0)),
            ],
            out_specs=pl.BlockSpec((16, ROWS, width + 128), lambda c, *_: (0, 0, 0)),
            scratch_shapes=[pltpu.VMEM((384, width), F32)],
        ),
        out_shape=jax.ShapeDtypeStruct((16, ROWS, width + 128), BF),
        compiler_params=pltpu.CompilerParams(vmem_limit_bytes=VMEM),
        cost_estimate=pl.CostEstimate(
            flops=4 * 384 * 6144 * width, transcendentals=0, bytes_accessed=6 << 20
        ),
        name=f"phase_{first}",
    )(where, momenta, own, other)


def source_kernel(
    where_ref, tau_ref, src_ref, mom_ref, gam_ref, ltab_ref, rtab_ref, out_ref, left_ref, right_ref
):
    n = pl.program_id(0)
    x = jnp.concatenate([tau_ref[:, 0].reshape(384, 384), tau_ref[:, 1].reshape(384, 384)], 1)
    s_real = src_ref[0, 0]
    s_imag = src_ref[0, 1]
    to_real = jnp.concatenate([s_real, s_imag], 1)
    to_imag = jnp.concatenate([s_imag, -s_real], 1)
    out_ref[:, 0, 0] = dot(x, to_real, 1, 1).astype(BF).reshape(ROWS, 16, 192)
    out_ref[:, 1, 0] = dot(x, to_imag, 1, 1).astype(BF).reshape(ROWS, 16, 192)

    @pl.when(n == 0)
    def _():
        chosen = (gam_ref[...] == lax.broadcasted_iota(jnp.int32, (64, 16), 1)).astype(BF)
        lane = lax.rem(lax.broadcasted_iota(jnp.int32, (64, 64), 1), MPAD)
        moment = mom_ref[...] == lane
        for a in range(4):
            for q in range(2):
                got = jnp.where(moment, dot(chosen, ltab_ref[q, a], 1, 0), 0.0)
                left_ref[q, 64 * a : 64 * a + 64, :] = got
        lane = lax.broadcasted_iota(jnp.int32, (64, 144), 1)
        low = mom_ref[...] * 16
        moment = jnp.logical_and(lane >= low, lane < low + 16)
        for y in range(4):
            for q in range(2):
                right_ref[q, y] = jnp.where(moment, dot(chosen, rtab_ref[q, y], 1, 0), 0.0)


def source_part(tau, source_blocks, op_momentum, op_gamma, where):
    ltab, rtab = spin_tables()
    whole = lambda shape: pl.BlockSpec(shape, lambda n, *_: (0,) * len(shape))
    return pl.pallas_call(
        source_kernel,
        grid_spec=pltpu.PrefetchScalarGridSpec(
            num_scalar_prefetch=1,
            grid=(NMOM,),
            in_specs=[
                whole((ROWS, 2, 16, 384)),
                pl.BlockSpec((1, 2, 192, 384), lambda n, w: (n, 0, lax.rem(w[0], 2), 0)),
                whole((64, 1)),
                whole((64, 1)),
                whole((2, 4, 16, 64)),
                whole((2, 4, 16, 144)),
            ],
            out_specs=[
                pl.BlockSpec((ROWS, 2, 1, 16, 192), lambda n, *_: (0, 0, n, 0, 0)),
                whole((2, 256, 64)),
                whole((2, 4, 64, 144)),
            ],
        ),
        out_shape=[
            jax.ShapeDtypeStruct((ROWS, 2, NMOM, 16, 192), BF),
            jax.ShapeDtypeStruct((2, 256, 64), F32),
            jax.ShapeDtypeStruct((2, 4, 64, 144), F32),
        ],
        compiler_params=pltpu.CompilerParams(vmem_limit_bytes=VMEM),
        cost_estimate=pl.CostEstimate(
            flops=8 * 384 * 384 * 1728, transcendentals=0, bytes_accessed=8 << 20
        ),
        name="source",
    )(
        where,
        tau,
        source_blocks,
        op_momentum[:, None],
        op_gamma[:, None],
        jnp.asarray(ltab, BF),
        jnp.asarray(rtab, BF),
    )


def sink_kernel(
    where_ref, own1, oth1, own2, oth2, tau_ref, src_ref, left_ref, right_ref, basis_ref, out_ref,
    rows_ref, sink_ref, acc_ref,
):
    core = lax.rem(where_ref[0], 2)
    rows_ref[...] = jnp.zeros_like(rows_ref)
    for c in range(2):
        one = jnp.where(core == c, own1[...], oth1[...]).astype(F32)
        two = jnp.where(core == c, own2[...], oth2[...]).astype(F32)
        for u in range(4):
            part = one if u < 2 else two
            for q in range(2):
                at = 768 * (u % 2) + 384 * q
                rows_ref[q, :, 4 * c + u, :] = part[:, at : at + 384]
        rows_ref[c, :, 8, :] = two[:, 1536:1920]
    real = rows_ref[0].reshape(384, 384).astype(BF)
    imag = rows_ref[1].reshape(384, 384).astype(BF)
    stacked = jnp.concatenate(
        [jnp.concatenate([real, -imag], 1), jnp.concatenate([imag, real], 1)], 0
    )
    for g in range(4):
        at = slice(768 * g, 768 * g + 768)
        here = jnp.concatenate([tau_ref[:, at], tau_ref[:, 3072 + 768 * g : 3840 + 768 * g]], 0)
        got = dot(stacked, here, 1, 0).astype(BF)
        for y in range(4):
            for q in range(2):
                sink_ref[q, 4 * y + g] = got[384 * q : 384 * q + 384, 192 * y : 192 * y + 192]
    acc_ref[...] = jnp.zeros_like(acc_ref)

    def one_row(r, carry):
        at = pl.ds(pl.multiple_of(r * MPAD, MPAD), MPAD)
        left = jnp.concatenate([sink_ref[q, :, at, :].reshape(256, 192) for q in range(2)], 0)
        right = src_ref[r].reshape(288, 192)
        acc_ref[...] += dot(left, right, 1, 1)
        return carry

    lax.fori_loop(0, ROWS, one_row, 0)
    acc = acc_ref[...]
    block_real = acc[:256, :144] - acc[256:, 144:]
    block_imag = acc[:256, 144:] + acc[256:, :144]
    l_real = left_ref[0]
    l_imag = left_ref[1]
    lifted = jnp.concatenate(
        [jnp.concatenate([l_real, -l_imag], 1), jnp.concatenate([l_imag, l_real], 1)], 0
    )
    spin = lax.rem(lax.broadcasted_iota(jnp.int32, (64, 144), 1), 16) // 4
    corr_real = jnp.zeros((64, 64), F32)
    corr_imag = jnp.zeros((64, 64), F32)
    for y in range(4):
        at = slice(64 * y, 64 * y + 64)
        both = jnp.concatenate([block_real[at], block_imag[at]], 0)
        got = dot(lifted, both, 1, 0, full_precision)
        halves = []
        for q in range(2):
            total = jnp.zeros((64, 144), F32)
            for a in range(4):
                low = 256 * q + 64 * a
                total = jnp.where(spin == a, got[low : low + 64], total)
            halves.append(total)
        r_real = right_ref[0, y]
        r_imag = right_ref[1, y]
        corr_real += dot(halves[0], r_real, 1, 1, full_precision)
        corr_real -= dot(halves[1], r_imag, 1, 1, full_precision)
        corr_imag += dot(halves[0], r_imag, 1, 1, full_precision)
        corr_imag += dot(halves[1], r_real, 1, 1, full_precision)
    b_real = basis_ref[0]
    b_imag = basis_ref[1]
    exact = functools.partial(dot, precision=full_precision)
    half_real = exact(corr_real, b_real, 1, 0) - exact(corr_imag, b_imag, 1, 0)
    half_imag = exact(corr_real, b_imag, 1, 0) + exact(corr_imag, b_real, 1, 0)
    out_ref[:64, :64] = corr_real
    out_ref[:64, 64:] = corr_imag
    out_ref[64:, :] = jnp.zeros((8, 128), F32)
    out_ref[64:, :8] = exact(b_real, half_real, 0, 0) + exact(b_imag, half_imag, 0, 0)
    out_ref[64:, 8:16] = exact(b_real, half_imag, 0, 0) - exact(b_imag, half_real, 0, 0)


def sink_part(where, own1, oth1, own2, oth2, tau, src, left, right, basis):
    specs = [pl.BlockSpec(memory_space=pltpu.VMEM)] * 9
    return pl.pallas_call(
        sink_kernel,
        grid_spec=pltpu.PrefetchScalarGridSpec(
            num_scalar_prefetch=1,
            grid=(),
            in_specs=specs,
            out_specs=pl.BlockSpec(memory_space=pltpu.VMEM),
            scratch_shapes=[
                pltpu.VMEM((2, ROWS, MPAD, 384), F32),
                pltpu.VMEM((2, 16, 384, 192), BF),
                pltpu.VMEM((512, 288), F32),
            ],
        ),
        out_shape=jax.ShapeDtypeStruct((72, 128), F32),
        compiler_params=pltpu.CompilerParams(vmem_limit_bytes=VMEM),
        name="sink",
    )(where, own1, oth1, own2, oth2, tau, src, left, right, basis)


def around(shard, axis):
    sent = [lax.ppermute(shard, "gx", shift(*(axis * d))) for d in (1, 3, 2)]
    return shard + sent[0] + sent[1] + sent[2]


def exchanged(part):
    return lax.all_to_all(part, "gx", 0, 0, tiled=True, axis_index_groups=SAME_CORE)


def summed(got, chip):
    total = jnp.sum(got.astype(F32), 0)
    width = total.shape[1] - 128
    lane = lax.broadcasted_iota(jnp.int32, (ROWS, width), 1)
    row = lax.broadcasted_iota(jnp.int32, (ROWS, width), 0)
    rest = jnp.zeros((ROWS, width), F32)
    for b in range(width // 384):
        diagonal = lane == 384 * b + ROWS * chip + row
        rest = jnp.where(diagonal, total[:, width + b : width + b + 1], rest)
    return (total[:, :width] + rest).astype(BF)


def body(eigvecs, perambulators, source_blocks, momenta, op_momentum, op_gamma, ref_vectors):
    device = lax.axis_index("gx")
    core = device % 2
    where = device[None]
    own = jnp.transpose(eigvecs.reshape(-1, 2, 384), (1, 0, 2))
    other = lax.ppermute(own, "gx", PAIR)
    mine = jnp.transpose(perambulators[0], (1, 0, 2, 3, 4)).reshape(12, 2, 16, 384)
    theirs = lax.ppermute(mine, "gx", PAIR)
    tau = jnp.where(
        core == 0, jnp.concatenate([mine, theirs], 0), jnp.concatenate([theirs, mine], 0)
    )
    part = jnp.where(core == 0, tau[..., :192], tau[..., 192:]).reshape(ROWS, 6144)
    tau_all = lax.all_gather(part, "gx", axis=0, tiled=True, axis_index_groups=SAME_CORE)
    flat = momenta.reshape(-1)
    first = phase_part(own, other, where, flat, 2, 2, 1)
    got2 = exchanged(first)
    second = phase_part(own, other, where, flat, 0, 2, 0)
    tau, second = lax.optimization_barrier((tau, second))
    got1 = exchanged(second)
    src, left, right = source_part(tau, source_blocks, op_momentum, op_gamma, where)
    got1, got2, src = lax.optimization_barrier((got1, got2, src))
    own1 = summed(got1, device // 2)
    own2 = summed(got2, device // 2)
    oth1 = lax.ppermute(own1, "gx", PAIR)
    oth2 = lax.ppermute(own2, "gx", PAIR)
    corr = sink_part(where, own1, oth1, own2, oth2, tau_all, src, left, right, ref_vectors)
    corr = corr + lax.ppermute(corr, "gx", PAIR)
    raw = corr[64:]
    first_raw = jnp.where(lax.axis_index("ta") == 0, raw, 0.0)
    for t in (1, 3, 2):
        first_raw = first_raw + lax.ppermute(raw, "ta", [(0, t)])
    corr = jnp.concatenate([corr, first_raw], 0)
    corr = around(corr, np.array([1, 0]))
    corr = around(corr, np.array([0, 1]))
    first_raw = corr[72:]
    scale_factor = lax.rsqrt(jnp.sum(first_raw * first_raw) * (1.0 / 128.0) + 1e-06)
    correlator = jnp.stack([corr[:64, :64], corr[:64, 64:]])[None]
    raw = jnp.stack([corr[64:72, :8], corr[64:72, 8:16]])
    return (correlator, (raw * scale_factor)[None])


def solution(mesh):
    placed = (
        P("ta", "gx", None, None, None),
        P("ta", None, "gx", None, None, None),
        P(),
        P(),
        P(),
        P(),
        P(),
    )
    return jax.shard_map(
        body,
        mesh=mesh,
        in_specs=placed,
        out_specs=(P("ta", None, None, None), P("ta", None, None, None)),
        check_vma=False,
    )
```

```python
import functools
import math

import jax
import jax.numpy as jnp
import numpy as np
from jax import lax
from jax.experimental import pallas as pl
from jax.experimental.pallas import tpu as pltpu
from jax.sharding import PartitionSpec as P

EXTENT = 96
NMOM = 9
BF = jnp.bfloat16
F32 = jnp.float32
HALF_PERIOD = -2.0 * math.pi / EXTENT
CHUNK = 768
ROWS = 24
MPAD = 16
VMEM = 60 << 20
full_precision = lax.Precision.HIGHEST
SAME_CORE = [[d for d in range(32) if d % 2 == c] for c in range(2)]
PAIR = [(d, d ^ 1) for d in range(32)]


def shift(x, z):
    ring = [(i, j, c) for i in range(4) for j in range(4) for c in range(2)]
    number = lambda i, j, c: i % 4 * 8 + j % 4 * 2 + c
    return [(number(i, j, c), number(i + x, j + z, c)) for i, j, c in ring]


def gamma_tables():
    zero_block = np.zeros((4, 4), np.float32)
    first_imag = np.array([[0, 0, 0, 1], [0, 0, 1, 0], [0, -1, 0, 0], [-1, 0, 0, 0]], np.float32)
    second_real = np.array([[0, 0, 0, -1], [0, 0, 1, 0], [0, 1, 0, 0], [-1, 0, 0, 0]], np.float32)
    third_imag = np.array([[0, 0, 1, 0], [0, 0, 0, -1], [-1, 0, 0, 0], [0, 1, 0, 0]], np.float32)
    fourth_real = np.array([[0, 0, 1, 0], [0, 0, 0, 1], [1, 0, 0, 0], [0, 1, 0, 0]], np.float32)
    gamma_list = [
        (zero_block, first_imag),
        (second_real, zero_block),
        (zero_block, third_imag),
        (fourth_real, zero_block),
    ]
    real_parts = []
    imag_parts = []
    for subset in range(16):
        prod_real = np.eye(4, dtype=np.float32)
        prod_imag = np.zeros((4, 4), np.float32)
        for position in range(4):
            if subset >> position & 1:
                factor_real, factor_imag = gamma_list[position]
                prod_real, prod_imag = (
                    prod_real @ factor_real - prod_imag @ factor_imag,
                    prod_real @ factor_imag + prod_imag @ factor_real,
                )
        real_parts.append(prod_real)
        imag_parts.append(prod_imag)
    return (np.stack(real_parts).astype(np.float32), np.stack(imag_parts).astype(np.float32))


def spin_tables():
    chiral = np.array([1.0, 1.0, -1.0, -1.0], np.float32)
    parts = np.stack(gamma_tables())
    left = np.transpose(parts, (0, 2, 1, 3)) * chiral[None, :, None, None]
    left = np.repeat(left[..., None], MPAD, -1).reshape(2, 4, 16, 4 * MPAD)
    right = np.transpose(parts, (0, 3, 1, 2)) * chiral
    right = right * np.array([1.0, -1.0], np.float32)[:, None, None, None]
    right = np.broadcast_to(right[:, :, :, None, None, :], (2, 4, 16, NMOM, 4, 4))
    return left, right.reshape(2, 4, 16, NMOM * 16)


def dot(left, right, lc, rc, precision=None):
    return lax.dot_general(
        left, right, (((lc,), (rc,)), ((), ())), precision=precision, preferred_element_type=F32
    )


def phase_kernel(first, full, half, steps, where_ref, mom_ref, own_ref, other_ref, out_ref, acc_ref):
    step = pl.program_id(0)
    core = lax.rem(where_ref[0], 2)
    is_own = step < steps
    real = jnp.where(is_own, own_ref[0], other_ref[0])
    imag = jnp.where(is_own, own_ref[1], other_ref[1])
    left = jnp.concatenate([real.T, imag.T], 1)
    device = jnp.where(is_own, where_ref[0], where_ref[0] + 1 - 2 * core)
    unit = lax.broadcasted_iota(jnp.int32, (8, CHUNK), 0)
    row = lax.rem(step, steps) * CHUNK + lax.broadcasted_iota(jnp.int32, (8, CHUNK), 1)
    site = jnp.floor((row.astype(F32) + 0.5) * (1.0 / 3.0)) + (device * 512).astype(F32)
    line = jnp.floor((site + 0.5) * (1.0 / EXTENT))
    xcoord = site - EXTENT * line
    zcoord = jnp.floor((line + 0.5) * (1.0 / EXTENT))
    ycoord = line - EXTENT * zcoord
    winding = jnp.zeros((8, CHUNK), F32)
    for u in range(full + half):
        m = 4 * core + first + u if u < full else NMOM - 1
        here = (
            mom_ref[3 * m].astype(F32) * xcoord
            + mom_ref[3 * m + 1].astype(F32) * ycoord
            + mom_ref[3 * m + 2].astype(F32) * zcoord
        )
        winding = jnp.where(unit == u, here, winding)
    winding = winding - EXTENT * jnp.floor((winding + 0.5) * (1.0 / EXTENT))
    angle = winding * HALF_PERIOD
    cosine = jnp.cos(angle)
    sine = jnp.sin(angle)
    if half:
        turned = jnp.logical_and(unit == full, core == 1)
        cosine, sine = jnp.where(turned, sine, cosine), jnp.where(turned, -cosine, sine)
    cosine = cosine.T
    sine = sine.T
    real = real.astype(F32)
    imag = imag.astype(F32)

    @pl.when(step == 0)
    def _():
        acc_ref[...] = jnp.zeros_like(acc_ref)

    for u in range(full + half):
        c = cosine[:, u : u + 1]
        s = sine[:, u : u + 1]
        twist_real = (c * real - s * imag).astype(BF)
        twist_imag = (c * imag + s * real).astype(BF)
        if u < full:
            right = jnp.concatenate(
                [
                    jnp.concatenate([twist_real, twist_imag], 1),
                    jnp.concatenate([twist_imag, -twist_real], 1),
                ],
                0,
            )
        else:
            right = jnp.concatenate([twist_real, twist_imag], 0)
        at = slice(768 * u, 768 * u + right.shape[1])
        acc_ref[:, at] += dot(left, right, 1, 0)

    @pl.when(step == 2 * steps - 1)
    def _():
        width = acc_ref.shape[1]
        diagonal = lax.broadcasted_iota(jnp.int32, (384, 384), 0) == lax.broadcasted_iota(
            jnp.int32, (384, 384), 1
        )
        lane = lax.broadcasted_iota(jnp.int32, (384, 128), 1)
        rest = jnp.zeros((384, 128), F32)
        for b in range(width // 384):
            block = acc_ref[:, 384 * b : 384 * b + 384]
            lost = jnp.where(diagonal, block - block.astype(BF).astype(F32), 0.0)
            rest = jnp.where(lane == b, jnp.sum(lost, 1, keepdims=True), rest)
        for j in range(16):
            at = slice(ROWS * j, ROWS * (j + 1))
            out_ref[j, :, :width] = acc_ref[at, :].astype(BF)
            out_ref[j, :, width:] = rest[at].astype(BF)


def phase_part(own, other, where, momenta, first, full, half):
    steps = own.shape[1] // CHUNK
    width = 768 * full + 384 * half
    return pl.pallas_call(
        functools.partial(phase_kernel, first, full, half, steps),
        grid_spec=pltpu.PrefetchScalarGridSpec(
            num_scalar_prefetch=2,
            grid=(2 * steps,),
            in_specs=[
                pl.BlockSpec((2, CHUNK, 384), lambda c, *_: (0, jnp.minimum(c, steps - 1), 0)),
                pl.BlockSpec((2, CHUNK, 384), lambda c, *_: (0, jnp.maximum(c - steps, 0), 0)),
            ],
            out_specs=pl.BlockSpec((16, ROWS, width + 128), lambda c, *_: (0, 0, 0)),
            scratch_shapes=[pltpu.VMEM((384, width), F32)],
        ),
        out_shape=jax.ShapeDtypeStruct((16, ROWS, width + 128), BF),
        compiler_params=pltpu.CompilerParams(vmem_limit_bytes=VMEM),
        cost_estimate=pl.CostEstimate(
            flops=4 * 384 * 6144 * width, transcendentals=0, bytes_accessed=6 << 20
        ),
        name=f"phase_{first}",
    )(where, momenta, own, other)


def source_kernel(
    where_ref, tau_ref, src_ref, mom_ref, gam_ref, ltab_ref, rtab_ref, vec_ref,
    out_ref, left_ref, right_ref, basis_ref,
):
    n = pl.program_id(0)
    x = jnp.concatenate([tau_ref[:, 0].reshape(384, 384), tau_ref[:, 1].reshape(384, 384)], 1)
    s_real = src_ref[0, 0]
    s_imag = src_ref[0, 1]
    to_real = jnp.concatenate([s_real, s_imag], 1)
    to_imag = jnp.concatenate([s_imag, -s_real], 1)
    out_ref[:, 0, 0] = dot(x, to_real, 1, 1).astype(BF).reshape(ROWS, 16, 192)
    out_ref[:, 1, 0] = dot(x, to_imag, 1, 1).astype(BF).reshape(ROWS, 16, 192)

    @pl.when(n == 0)
    def _():
        basis_ref[...] = vec_ref[...]
        chosen = (gam_ref[...] == lax.broadcasted_iota(jnp.int32, (64, 16), 1)).astype(BF)
        lane = lax.rem(lax.broadcasted_iota(jnp.int32, (64, 64), 1), MPAD)
        moment = mom_ref[...] == lane
        for a in range(4):
            for q in range(2):
                got = jnp.where(moment, dot(chosen, ltab_ref[q, a], 1, 0), 0.0)
                left_ref[q, 64 * a : 64 * a + 64, :] = got
        lane = lax.broadcasted_iota(jnp.int32, (64, 144), 1)
        low = mom_ref[...] * 16
        moment = jnp.logical_and(lane >= low, lane < low + 16)
        for y in range(4):
            for q in range(2):
                right_ref[q, y] = jnp.where(moment, dot(chosen, rtab_ref[q, y], 1, 0), 0.0)


def source_part(tau, source_blocks, op_momentum, op_gamma, ref_vectors, where):
    ltab, rtab = spin_tables()
    whole = lambda shape: pl.BlockSpec(shape, lambda n, *_: (0,) * len(shape))
    return pl.pallas_call(
        source_kernel,
        grid_spec=pltpu.PrefetchScalarGridSpec(
            num_scalar_prefetch=1,
            grid=(NMOM,),
            in_specs=[
                whole((ROWS, 2, 16, 384)),
                pl.BlockSpec((1, 2, 192, 384), lambda n, w: (n, 0, lax.rem(w[0], 2), 0)),
                whole((64, 1)),
                whole((64, 1)),
                whole((2, 4, 16, 64)),
                whole((2, 4, 16, 144)),
                whole((2, 64, 8)),
            ],
            out_specs=[
                pl.BlockSpec((ROWS, 2, 1, 16, 192), lambda n, *_: (0, 0, n, 0, 0)),
                whole((2, 256, 64)),
                whole((2, 4, 64, 144)),
                whole((2, 64, 8)),
            ],
        ),
        out_shape=[
            jax.ShapeDtypeStruct((ROWS, 2, NMOM, 16, 192), BF),
            jax.ShapeDtypeStruct((2, 256, 64), F32),
            jax.ShapeDtypeStruct((2, 4, 64, 144), F32),
            jax.ShapeDtypeStruct((2, 64, 8), F32),
        ],
        compiler_params=pltpu.CompilerParams(vmem_limit_bytes=VMEM),
        cost_estimate=pl.CostEstimate(
            flops=8 * 384 * 384 * 1728, transcendentals=0, bytes_accessed=8 << 20
        ),
        name="source",
    )(
        where,
        tau,
        source_blocks,
        op_momentum[:, None],
        op_gamma[:, None],
        jnp.asarray(ltab, BF),
        jnp.asarray(rtab, BF),
        ref_vectors,
    )


def thirds(value):
    high = value.astype(BF)
    rest = value - high.astype(F32)
    middle = rest.astype(BF)
    return [high, middle, (rest - middle.astype(F32)).astype(BF)]


def sink_kernel(
    where_ref, own1, oth1, own2, oth2, tau_hbm, src_hbm, left_ref, right_ref, basis_ref, out_ref,
    rows_ref, sink_ref, acc_ref, tau_ref, src_ref, sem,
):
    core = lax.rem(where_ref[0], 2)
    fetches = []
    for g in range(4):
        for q in range(2):
            source = tau_hbm.at[:, pl.ds(3072 * q + 768 * g, 768)]
            target = tau_ref.at[q, :, pl.ds(768 * g, 768)]
            fetches.append(pltpu.make_async_copy(source, target, sem.at[2 * g + q]))
    fetches.append(pltpu.make_async_copy(src_hbm, src_ref, sem.at[8]))
    for fetch in fetches:
        fetch.start()
    rows_ref[...] = jnp.zeros_like(rows_ref)
    for c in range(2):
        one = jnp.where(core == c, own1[...], oth1[...]).astype(F32)
        two = jnp.where(core == c, own2[...], oth2[...]).astype(F32)
        for u in range(4):
            part = one if u < 2 else two
            for q in range(2):
                at = 768 * (u % 2) + 384 * q
                rows_ref[q, :, 4 * c + u, :] = part[:, at : at + 384]
        rows_ref[c, :, 8, :] = two[:, 1536:1920]
    real = rows_ref[0].reshape(384, 384).astype(BF)
    imag = rows_ref[1].reshape(384, 384).astype(BF)
    stacked = jnp.concatenate(
        [jnp.concatenate([real, -imag], 1), jnp.concatenate([imag, real], 1)], 0
    )
    for g in range(4):
        fetches[2 * g].wait()
        fetches[2 * g + 1].wait()
        at = slice(768 * g, 768 * g + 768)
        here = jnp.concatenate([tau_ref[0, :, at], tau_ref[1, :, at]], 0)
        got = dot(stacked, here, 1, 0).astype(BF)
        for y in range(4):
            for q in range(2):
                sink_ref[q, 4 * y + g] = got[384 * q : 384 * q + 384, 192 * y : 192 * y + 192]
    acc_ref[...] = jnp.zeros_like(acc_ref)
    fetches[8].wait()

    def one_row(r, carry):
        at = pl.ds(pl.multiple_of(r * MPAD, MPAD), MPAD)
        left = jnp.concatenate([sink_ref[q, :, at, :].reshape(256, 192) for q in range(2)], 0)
        right = src_ref[r].reshape(288, 192)
        acc_ref[...] += dot(right, left, 1, 1)
        return carry

    lax.fori_loop(0, ROWS, one_row, 0, unroll=8)
    acc = acc_ref[...]
    block_real = acc[:144, :256] - acc[144:, 256:]
    block_imag = acc[144:, :256] + acc[:144, 256:]
    l_real = left_ref[0]
    l_imag = left_ref[1]
    lifted = jnp.concatenate(
        [jnp.concatenate([l_real, -l_imag], 1), jnp.concatenate([l_imag, l_real], 1)], 0
    ).astype(BF)
    lifted = jnp.concatenate([lifted] * 3, 1)
    spin = lax.rem(lax.broadcasted_iota(jnp.int32, (64, 144), 1), 16) // 4
    corr_real = jnp.zeros((64, 64), F32)
    corr_imag = jnp.zeros((64, 64), F32)
    for y in range(4):
        at = slice(64 * y, 64 * y + 64)
        both = thirds(jnp.concatenate([block_real[:, at], block_imag[:, at]], 1))
        got = dot(lifted, jnp.concatenate(both, 1), 1, 1)
        halves = []
        for q in range(2):
            total = jnp.zeros((64, 144), F32)
            for a in range(4):
                low = 256 * q + 64 * a
                total = jnp.where(spin == a, got[low : low + 64], total)
            halves.append(total)
        r_real = right_ref[0, y]
        r_imag = right_ref[1, y]
        weights = jnp.concatenate([r_real, r_imag], 0).astype(BF)
        lhs = jnp.concatenate(thirds(jnp.concatenate(halves, 0)), 0)
        got = dot(lhs, weights, 1, 1)
        got = got[:128] + got[128:256] + got[256:]
        corr_real += got[:64, :64] - got[64:, 64:]
        corr_imag += got[:64, 64:] + got[64:, :64]
    b_real = basis_ref[0]
    b_imag = basis_ref[1]
    exact = functools.partial(dot, precision=full_precision)
    half_real = exact(corr_real, b_real, 1, 0) - exact(corr_imag, b_imag, 1, 0)
    half_imag = exact(corr_real, b_imag, 1, 0) + exact(corr_imag, b_real, 1, 0)
    out_ref[:64, :64] = corr_real
    out_ref[:64, 64:] = corr_imag
    out_ref[64:, :] = jnp.zeros((8, 128), F32)
    out_ref[64:, :8] = exact(b_real, half_real, 0, 0) + exact(b_imag, half_imag, 0, 0)
    out_ref[64:, 8:16] = exact(b_real, half_imag, 0, 0) - exact(b_imag, half_real, 0, 0)


def sink_part(where, own1, oth1, own2, oth2, tau, src, left, right, basis):
    inside = pl.BlockSpec(memory_space=pltpu.VMEM)
    outside = pl.BlockSpec(memory_space=pl.ANY)
    specs = [inside] * 4 + [outside] * 2 + [inside] * 3
    return pl.pallas_call(
        sink_kernel,
        grid_spec=pltpu.PrefetchScalarGridSpec(
            num_scalar_prefetch=1,
            grid=(),
            in_specs=specs,
            out_specs=pl.BlockSpec(memory_space=pltpu.VMEM),
            scratch_shapes=[
                pltpu.VMEM((2, ROWS, MPAD, 384), F32),
                pltpu.VMEM((2, 16, 384, 192), BF),
                pltpu.VMEM((288, 512), F32),
                pltpu.VMEM((2, 384, 3072), BF),
                pltpu.VMEM((ROWS, 2, NMOM, 16, 192), BF),
                pltpu.SemaphoreType.DMA((9,)),
            ],
        ),
        out_shape=jax.ShapeDtypeStruct((72, 128), F32),
        compiler_params=pltpu.CompilerParams(vmem_limit_bytes=VMEM),
        name="sink",
    )(where, own1, oth1, own2, oth2, tau, src, left, right, basis)


def around(shard, axis):
    sent = [lax.ppermute(shard, "gx", shift(*(axis * d))) for d in (1, 3, 2)]
    return shard + sent[0] + sent[1] + sent[2]


def exchanged(part):
    return lax.all_to_all(part, "gx", 0, 0, tiled=True, axis_index_groups=SAME_CORE)


def summed(got, chip):
    total = jnp.sum(got.astype(F32), 0)
    width = total.shape[1] - 128
    lane = lax.broadcasted_iota(jnp.int32, (ROWS, width), 1)
    row = lax.broadcasted_iota(jnp.int32, (ROWS, width), 0)
    rest = jnp.zeros((ROWS, width), F32)
    for b in range(width // 384):
        diagonal = lane == 384 * b + ROWS * chip + row
        rest = jnp.where(diagonal, total[:, width + b : width + b + 1], rest)
    return (total[:, :width] + rest).astype(BF)


def body(eigvecs, perambulators, source_blocks, momenta, op_momentum, op_gamma, ref_vectors):
    device = lax.axis_index("gx")
    core = device % 2
    where = device[None]
    own = jnp.transpose(eigvecs.reshape(-1, 2, 384), (1, 0, 2))
    own, perambulators = lax.optimization_barrier((own, perambulators))
    other = lax.ppermute(own, "gx", PAIR)
    mine = jnp.transpose(perambulators[0], (1, 0, 2, 3, 4)).reshape(12, 2, 16, 384)
    theirs = lax.ppermute(mine, "gx", PAIR)
    tau = jnp.where(
        core == 0, jnp.concatenate([mine, theirs], 0), jnp.concatenate([theirs, mine], 0)
    )
    part = jnp.where(core == 0, tau[..., :192], tau[..., 192:]).reshape(ROWS, 6144)
    tau_all = lax.all_gather(part, "gx", axis=0, tiled=True, axis_index_groups=SAME_CORE)
    flat = momenta.reshape(-1)
    first = phase_part(own, other, where, flat, 2, 2, 1)
    got2 = exchanged(first)
    second = phase_part(own, other, where, flat, 0, 2, 0)
    tau, second = lax.optimization_barrier((tau, second))
    got1 = exchanged(second)
    src, left, right, basis = source_part(
        tau, source_blocks, op_momentum, op_gamma, ref_vectors, where
    )
    got1, got2, src = lax.optimization_barrier((got1, got2, src))
    own1 = summed(got1, device // 2)
    own2 = summed(got2, device // 2)
    oth1 = lax.ppermute(own1, "gx", PAIR)
    oth2 = lax.ppermute(own2, "gx", PAIR)
    corr = sink_part(where, own1, oth1, own2, oth2, tau_all, src, left, right, basis)
    corr = corr + lax.ppermute(corr, "gx", PAIR)
    raw = corr[64:]
    first_raw = jnp.where(lax.axis_index("ta") == 0, raw, 0.0)
    for t in (1, 3, 2):
        first_raw = first_raw + lax.ppermute(raw, "ta", [(0, t)])
    corr = jnp.concatenate([corr, first_raw], 0)
    corr = around(corr, np.array([1, 0]))
    corr = around(corr, np.array([0, 1]))
    first_raw = corr[72:]
    scale_factor = lax.rsqrt(jnp.sum(first_raw * first_raw) * (1.0 / 128.0) + 1e-06)
    correlator = jnp.stack([corr[:64, :64], corr[:64, 64:]])[None]
    raw = jnp.stack([corr[64:72, :8], corr[64:72, 8:16]])
    return (correlator, (raw * scale_factor)[None])


def solution(mesh):
    placed = (
        P("ta", "gx", None, None, None),
        P("ta", None, "gx", None, None, None),
        P(),
        P(),
        P(),
        P(),
        P(),
    )
    return jax.shard_map(
        body,
        mesh=mesh,
        in_specs=placed,
        out_specs=(P("ta", None, None, None), P("ta", None, None, None)),
        check_vma=False,
    )
```

```python
import functools
import math

import jax
import jax.numpy as jnp
import numpy as np
from jax import lax
from jax.experimental import pallas as pl
from jax.experimental.pallas import tpu as pltpu
from jax.sharding import PartitionSpec as P

EXTENT = 96
NMOM = 9
BF = jnp.bfloat16
F32 = jnp.float32
HALF_PERIOD = -2.0 * math.pi / EXTENT
CHUNK = 768
ROWS = 24
MPAD = 16
VMEM = 60 << 20
full_precision = lax.Precision.HIGHEST
SAME_CORE = [[d for d in range(32) if d % 2 == c] for c in range(2)]
PAIR = [(d, d ^ 1) for d in range(32)]


def shift(x, z):
    ring = [(i, j, c) for i in range(4) for j in range(4) for c in range(2)]
    number = lambda i, j, c: i % 4 * 8 + j % 4 * 2 + c
    return [(number(i, j, c), number(i + x, j + z, c)) for i, j, c in ring]


def gamma_tables():
    zero_block = np.zeros((4, 4), np.float32)
    first_imag = np.array([[0, 0, 0, 1], [0, 0, 1, 0], [0, -1, 0, 0], [-1, 0, 0, 0]], np.float32)
    second_real = np.array([[0, 0, 0, -1], [0, 0, 1, 0], [0, 1, 0, 0], [-1, 0, 0, 0]], np.float32)
    third_imag = np.array([[0, 0, 1, 0], [0, 0, 0, -1], [-1, 0, 0, 0], [0, 1, 0, 0]], np.float32)
    fourth_real = np.array([[0, 0, 1, 0], [0, 0, 0, 1], [1, 0, 0, 0], [0, 1, 0, 0]], np.float32)
    gamma_list = [
        (zero_block, first_imag),
        (second_real, zero_block),
        (zero_block, third_imag),
        (fourth_real, zero_block),
    ]
    real_parts = []
    imag_parts = []
    for subset in range(16):
        prod_real = np.eye(4, dtype=np.float32)
        prod_imag = np.zeros((4, 4), np.float32)
        for position in range(4):
            if subset >> position & 1:
                factor_real, factor_imag = gamma_list[position]
                prod_real, prod_imag = (
                    prod_real @ factor_real - prod_imag @ factor_imag,
                    prod_real @ factor_imag + prod_imag @ factor_real,
                )
        real_parts.append(prod_real)
        imag_parts.append(prod_imag)
    return (np.stack(real_parts).astype(np.float32), np.stack(imag_parts).astype(np.float32))


def spin_tables():
    chiral = np.array([1.0, 1.0, -1.0, -1.0], np.float32)
    parts = np.stack(gamma_tables())
    left = np.transpose(parts, (0, 2, 1, 3)) * chiral[None, :, None, None]
    left = np.repeat(left[..., None], MPAD, -1).reshape(2, 4, 16, 4 * MPAD)
    right = np.transpose(parts, (0, 3, 1, 2)) * chiral
    right = right * np.array([1.0, -1.0], np.float32)[:, None, None, None]
    right = np.broadcast_to(right[:, :, :, None, None, :], (2, 4, 16, NMOM, 4, 4))
    return left, right.reshape(2, 4, 16, NMOM * 16)


def dot(left, right, lc, rc, precision=None):
    return lax.dot_general(
        left, right, (((lc,), (rc,)), ((), ())), precision=precision, preferred_element_type=F32
    )


def phase_kernel(first, full, half, steps, where_ref, mom_ref, own_ref, other_ref, out_ref, acc_ref):
    step = pl.program_id(0)
    core = lax.rem(where_ref[0], 2)
    is_own = step < steps
    real = jnp.where(is_own, own_ref[0], other_ref[0])
    imag = jnp.where(is_own, own_ref[1], other_ref[1])
    left = jnp.concatenate([real.T, imag.T], 1)
    device = jnp.where(is_own, where_ref[0], where_ref[0] + 1 - 2 * core)
    unit = lax.broadcasted_iota(jnp.int32, (8, CHUNK), 0)
    row = lax.rem(step, steps) * CHUNK + lax.broadcasted_iota(jnp.int32, (8, CHUNK), 1)
    site = jnp.floor((row.astype(F32) + 0.5) * (1.0 / 3.0)) + (device * 512).astype(F32)
    line = jnp.floor((site + 0.5) * (1.0 / EXTENT))
    xcoord = site - EXTENT * line
    zcoord = jnp.floor((line + 0.5) * (1.0 / EXTENT))
    ycoord = line - EXTENT * zcoord
    winding = jnp.zeros((8, CHUNK), F32)
    for u in range(full + half):
        m = 4 * core + first + u if u < full else NMOM - 1
        here = (
            mom_ref[3 * m].astype(F32) * xcoord
            + mom_ref[3 * m + 1].astype(F32) * ycoord
            + mom_ref[3 * m + 2].astype(F32) * zcoord
        )
        winding = jnp.where(unit == u, here, winding)
    winding = winding - EXTENT * jnp.floor((winding + 0.5) * (1.0 / EXTENT))
    angle = winding * HALF_PERIOD
    cosine = jnp.cos(angle)
    sine = jnp.sin(angle)
    if half:
        turned = jnp.logical_and(unit == full, core == 1)
        cosine, sine = jnp.where(turned, sine, cosine), jnp.where(turned, -cosine, sine)
    cosine = cosine.T
    sine = sine.T
    real = real.astype(F32)
    imag = imag.astype(F32)

    @pl.when(step == 0)
    def _():
        acc_ref[...] = jnp.zeros_like(acc_ref)

    for u in range(full + half):
        c = cosine[:, u : u + 1]
        s = sine[:, u : u + 1]
        twist_real = (c * real - s * imag).astype(BF)
        twist_imag = (c * imag + s * real).astype(BF)
        if u < full:
            right = jnp.concatenate(
                [
                    jnp.concatenate([twist_real, twist_imag], 1),
                    jnp.concatenate([twist_imag, -twist_real], 1),
                ],
                0,
            )
        else:
            right = jnp.concatenate([twist_real, twist_imag], 0)
        at = slice(768 * u, 768 * u + right.shape[1])
        acc_ref[:, at] += dot(left, right, 1, 0)

    @pl.when(step == 2 * steps - 1)
    def _():
        width = acc_ref.shape[1]
        diagonal = lax.broadcasted_iota(jnp.int32, (384, 384), 0) == lax.broadcasted_iota(
            jnp.int32, (384, 384), 1
        )
        lane = lax.broadcasted_iota(jnp.int32, (384, 128), 1)
        rest = jnp.zeros((384, 128), F32)
        for b in range(width // 384):
            block = acc_ref[:, 384 * b : 384 * b + 384]
            lost = jnp.where(diagonal, block - block.astype(BF).astype(F32), 0.0)
            rest = jnp.where(lane == b, jnp.sum(lost, 1, keepdims=True), rest)
        for j in range(16):
            at = slice(ROWS * j, ROWS * (j + 1))
            out_ref[j, :, :width] = acc_ref[at, :].astype(BF)
            out_ref[j, :, width:] = rest[at].astype(BF)


def phase_part(own, other, where, momenta, first, full, half):
    steps = own.shape[1] // CHUNK
    width = 768 * full + 384 * half
    return pl.pallas_call(
        functools.partial(phase_kernel, first, full, half, steps),
        grid_spec=pltpu.PrefetchScalarGridSpec(
            num_scalar_prefetch=2,
            grid=(2 * steps,),
            in_specs=[
                pl.BlockSpec((2, CHUNK, 384), lambda c, *_: (0, jnp.minimum(c, steps - 1), 0)),
                pl.BlockSpec((2, CHUNK, 384), lambda c, *_: (0, jnp.maximum(c - steps, 0), 0)),
            ],
            out_specs=pl.BlockSpec((16, ROWS, width + 128), lambda c, *_: (0, 0, 0)),
            scratch_shapes=[pltpu.VMEM((384, width), F32)],
        ),
        out_shape=jax.ShapeDtypeStruct((16, ROWS, width + 128), BF),
        compiler_params=pltpu.CompilerParams(vmem_limit_bytes=VMEM),
        cost_estimate=pl.CostEstimate(
            flops=4 * 384 * 6144 * width, transcendentals=0, bytes_accessed=6 << 20
        ),
        name=f"phase_{first}",
    )(where, momenta, own, other)


def source_kernel(
    where_ref, tau_ref, src_ref, mom_ref, gam_ref, ltab_ref, rtab_ref, vec_ref,
    out_ref, left_ref, right_ref, basis_ref,
):
    n = pl.program_id(0)
    x = jnp.concatenate([tau_ref[:, 0].reshape(384, 384), tau_ref[:, 1].reshape(384, 384)], 1)
    s_real = src_ref[0, 0]
    s_imag = src_ref[0, 1]
    to_real = jnp.concatenate([s_real, s_imag], 1)
    to_imag = jnp.concatenate([s_imag, -s_real], 1)
    out_ref[:, 0, 0] = dot(x, to_real, 1, 1).astype(BF).reshape(ROWS, 16, 192)
    out_ref[:, 1, 0] = dot(x, to_imag, 1, 1).astype(BF).reshape(ROWS, 16, 192)

    @pl.when(n == 0)
    def _():
        basis_ref[...] = vec_ref[...]
        chosen = (gam_ref[...] == lax.broadcasted_iota(jnp.int32, (64, 16), 1)).astype(BF)
        lane = lax.rem(lax.broadcasted_iota(jnp.int32, (64, 64), 1), MPAD)
        moment = mom_ref[...] == lane
        for a in range(4):
            for q in range(2):
                got = jnp.where(moment, dot(chosen, ltab_ref[q, a], 1, 0), 0.0)
                left_ref[q, 64 * a : 64 * a + 64, :] = got
        lane = lax.broadcasted_iota(jnp.int32, (64, 144), 1)
        low = mom_ref[...] * 16
        moment = jnp.logical_and(lane >= low, lane < low + 16)
        for y in range(4):
            for q in range(2):
                right_ref[q, y] = jnp.where(moment, dot(chosen, rtab_ref[q, y], 1, 0), 0.0)


def source_part(tau, source_blocks, op_momentum, op_gamma, ref_vectors, where):
    ltab, rtab = spin_tables()
    whole = lambda shape: pl.BlockSpec(shape, lambda n, *_: (0,) * len(shape))
    return pl.pallas_call(
        source_kernel,
        grid_spec=pltpu.PrefetchScalarGridSpec(
            num_scalar_prefetch=1,
            grid=(NMOM,),
            in_specs=[
                whole((ROWS, 2, 16, 384)),
                pl.BlockSpec((1, 2, 192, 384), lambda n, w: (n, 0, lax.rem(w[0], 2), 0)),
                whole((64, 1)),
                whole((64, 1)),
                whole((2, 4, 16, 64)),
                whole((2, 4, 16, 144)),
                whole((2, 64, 8)),
            ],
            out_specs=[
                pl.BlockSpec((ROWS, 2, 1, 16, 192), lambda n, *_: (0, 0, n, 0, 0)),
                whole((2, 256, 64)),
                whole((2, 4, 64, 144)),
                whole((2, 64, 8)),
            ],
        ),
        out_shape=[
            jax.ShapeDtypeStruct((ROWS, 2, NMOM, 16, 192), BF),
            jax.ShapeDtypeStruct((2, 256, 64), F32),
            jax.ShapeDtypeStruct((2, 4, 64, 144), F32),
            jax.ShapeDtypeStruct((2, 64, 8), F32),
        ],
        compiler_params=pltpu.CompilerParams(vmem_limit_bytes=VMEM),
        cost_estimate=pl.CostEstimate(
            flops=8 * 384 * 384 * 1728, transcendentals=0, bytes_accessed=8 << 20
        ),
        name="source",
    )(
        where,
        tau,
        source_blocks,
        op_momentum[:, None],
        op_gamma[:, None],
        jnp.asarray(ltab, BF),
        jnp.asarray(rtab, BF),
        ref_vectors,
    )


def thirds(value):
    high = value.astype(BF)
    rest = value - high.astype(F32)
    middle = rest.astype(BF)
    return [high, middle, (rest - middle.astype(F32)).astype(BF)]


def sink_kernel(
    where_ref, own1, oth1, own2, oth2, tau_hbm, src_hbm, left_ref, right_ref, basis_ref, out_ref,
    rows_ref, sink_ref, acc_ref, tau_ref, src_ref, sem,
):
    core = lax.rem(where_ref[0], 2)
    fetches = []
    for g in range(4):
        for q in range(2):
            source = tau_hbm.at[:, pl.ds(3072 * q + 768 * g, 768)]
            target = tau_ref.at[q, :, pl.ds(768 * g, 768)]
            fetches.append(pltpu.make_async_copy(source, target, sem.at[2 * g + q]))
    fetches.append(pltpu.make_async_copy(src_hbm, src_ref, sem.at[8]))
    for fetch in fetches:
        fetch.start()
    rows_ref[...] = jnp.zeros_like(rows_ref)
    for c in range(2):
        one = jnp.where(core == c, own1[...], oth1[...]).astype(F32)
        two = jnp.where(core == c, own2[...], oth2[...]).astype(F32)
        for u in range(4):
            part = one if u < 1 else two
            for q in range(2):
                at = 768 * max(u - 1, 0) + 384 * q
                rows_ref[q, :, 4 * c + u, :] = part[:, at : at + 384]
        rows_ref[c, :, 8, :] = one[:, 768:1152]
    real = rows_ref[0].reshape(384, 384).astype(BF)
    imag = rows_ref[1].reshape(384, 384).astype(BF)
    stacked = jnp.concatenate(
        [jnp.concatenate([real, -imag], 1), jnp.concatenate([imag, real], 1)], 0
    )
    for g in range(4):
        fetches[2 * g].wait()
        fetches[2 * g + 1].wait()
        at = slice(768 * g, 768 * g + 768)
        here = jnp.concatenate([tau_ref[0, :, at], tau_ref[1, :, at]], 0)
        got = dot(stacked, here, 1, 0).astype(BF)
        for y in range(4):
            for q in range(2):
                sink_ref[q, 4 * y + g] = got[384 * q : 384 * q + 384, 192 * y : 192 * y + 192]
    acc_ref[...] = jnp.zeros_like(acc_ref)
    fetches[8].wait()

    def one_row(r, carry):
        at = pl.ds(pl.multiple_of(r * MPAD, MPAD), MPAD)
        left = jnp.concatenate([sink_ref[q, :, at, :].reshape(256, 192) for q in range(2)], 0)
        right = src_ref[r].reshape(288, 192)
        acc_ref[...] += dot(right, left, 1, 1)
        return carry

    lax.fori_loop(0, ROWS, one_row, 0, unroll=8)
    acc = acc_ref[...]
    block_real = acc[:144, :256] - acc[144:, 256:]
    block_imag = acc[144:, :256] + acc[:144, 256:]
    l_real = left_ref[0]
    l_imag = left_ref[1]
    lifted = jnp.concatenate(
        [jnp.concatenate([l_real, -l_imag], 1), jnp.concatenate([l_imag, l_real], 1)], 0
    ).astype(BF)
    lifted = jnp.concatenate([lifted] * 3, 1)
    spin = lax.rem(lax.broadcasted_iota(jnp.int32, (64, 144), 1), 16) // 4
    corr_real = jnp.zeros((64, 64), F32)
    corr_imag = jnp.zeros((64, 64), F32)
    for y in range(4):
        at = slice(64 * y, 64 * y + 64)
        both = thirds(jnp.concatenate([block_real[:, at], block_imag[:, at]], 1))
        got = dot(lifted, jnp.concatenate(both, 1), 1, 1)
        halves = []
        for q in range(2):
            total = jnp.zeros((64, 144), F32)
            for a in range(4):
                low = 256 * q + 64 * a
                total = jnp.where(spin == a, got[low : low + 64], total)
            halves.append(total)
        r_real = right_ref[0, y]
        r_imag = right_ref[1, y]
        weights = jnp.concatenate([r_real, r_imag], 0).astype(BF)
        lhs = jnp.concatenate(thirds(jnp.concatenate(halves, 0)), 0)
        got = dot(lhs, weights, 1, 1)
        got = got[:128] + got[128:256] + got[256:]
        corr_real += got[:64, :64] - got[64:, 64:]
        corr_imag += got[:64, 64:] + got[64:, :64]
    b_real = basis_ref[0]
    b_imag = basis_ref[1]
    exact = functools.partial(dot, precision=full_precision)
    half_real = exact(corr_real, b_real, 1, 0) - exact(corr_imag, b_imag, 1, 0)
    half_imag = exact(corr_real, b_imag, 1, 0) + exact(corr_imag, b_real, 1, 0)
    out_ref[:64, :64] = corr_real
    out_ref[:64, 64:] = corr_imag
    out_ref[64:, :] = jnp.zeros((8, 128), F32)
    out_ref[64:, :8] = exact(b_real, half_real, 0, 0) + exact(b_imag, half_imag, 0, 0)
    out_ref[64:, 8:16] = exact(b_real, half_imag, 0, 0) - exact(b_imag, half_real, 0, 0)


def sink_part(where, own1, oth1, own2, oth2, tau, src, left, right, basis):
    inside = pl.BlockSpec(memory_space=pltpu.VMEM)
    outside = pl.BlockSpec(memory_space=pl.ANY)
    specs = [inside] * 4 + [outside] * 2 + [inside] * 3
    return pl.pallas_call(
        sink_kernel,
        grid_spec=pltpu.PrefetchScalarGridSpec(
            num_scalar_prefetch=1,
            grid=(),
            in_specs=specs,
            out_specs=pl.BlockSpec(memory_space=pltpu.VMEM),
            scratch_shapes=[
                pltpu.VMEM((2, ROWS, MPAD, 384), F32),
                pltpu.VMEM((2, 16, 384, 192), BF),
                pltpu.VMEM((288, 512), F32),
                pltpu.VMEM((2, 384, 3072), BF),
                pltpu.VMEM((ROWS, 2, NMOM, 16, 192), BF),
                pltpu.SemaphoreType.DMA((9,)),
            ],
        ),
        out_shape=jax.ShapeDtypeStruct((72, 128), F32),
        compiler_params=pltpu.CompilerParams(vmem_limit_bytes=VMEM),
        name="sink",
    )(where, own1, oth1, own2, oth2, tau, src, left, right, basis)


def around(shard, axis):
    sent = [lax.ppermute(shard, "gx", shift(*(axis * d))) for d in (1, 3, 2)]
    return shard + sent[0] + sent[1] + sent[2]


def exchanged(part):
    return lax.all_to_all(part, "gx", 0, 0, tiled=True, axis_index_groups=SAME_CORE)


def summed(got, chip):
    total = jnp.sum(got.astype(F32), 0)
    width = total.shape[1] - 128
    lane = lax.broadcasted_iota(jnp.int32, (ROWS, width), 1)
    row = lax.broadcasted_iota(jnp.int32, (ROWS, width), 0)
    rest = jnp.zeros((ROWS, width), F32)
    for b in range(width // 384):
        diagonal = lane == 384 * b + ROWS * chip + row
        rest = jnp.where(diagonal, total[:, width + b : width + b + 1], rest)
    return (total[:, :width] + rest).astype(BF)


def body(eigvecs, perambulators, source_blocks, momenta, op_momentum, op_gamma, ref_vectors):
    device = lax.axis_index("gx")
    core = device % 2
    where = device[None]
    own = jnp.transpose(eigvecs.reshape(-1, 2, 384), (1, 0, 2))
    own, perambulators = lax.optimization_barrier((own, perambulators))
    other = lax.ppermute(own, "gx", PAIR)
    mine = jnp.transpose(perambulators[0], (1, 0, 2, 3, 4)).reshape(12, 2, 16, 384)
    theirs = lax.ppermute(mine, "gx", PAIR)
    tau = jnp.where(
        core == 0, jnp.concatenate([mine, theirs], 0), jnp.concatenate([theirs, mine], 0)
    )
    part = jnp.where(core == 0, tau[..., :192], tau[..., 192:]).reshape(ROWS, 6144)
    tau_all = lax.all_gather(part, "gx", axis=0, tiled=True, axis_index_groups=SAME_CORE)
    flat = momenta.reshape(-1)
    first = phase_part(own, other, where, flat, 0, 1, 1)
    own, first = lax.optimization_barrier((own, first))
    got1 = exchanged(first)
    second = phase_part(own, other, where, flat, 1, 3, 0)
    tau, second = lax.optimization_barrier((tau, second))
    got2 = exchanged(second)
    src, left, right, basis = source_part(
        tau, source_blocks, op_momentum, op_gamma, ref_vectors, where
    )
    got1, got2, src = lax.optimization_barrier((got1, got2, src))
    own1 = summed(got1, device // 2)
    own2 = summed(got2, device // 2)
    oth1 = lax.ppermute(own1, "gx", PAIR)
    oth2 = lax.ppermute(own2, "gx", PAIR)
    corr = sink_part(where, own1, oth1, own2, oth2, tau_all, src, left, right, basis)
    corr = corr + lax.ppermute(corr, "gx", PAIR)
    raw = corr[64:]
    first_raw = jnp.where(lax.axis_index("ta") == 0, raw, 0.0)
    for t in (1, 3, 2):
        first_raw = first_raw + lax.ppermute(raw, "ta", [(0, t)])
    corr = jnp.concatenate([corr, first_raw], 0)
    corr = around(corr, np.array([1, 0]))
    corr = around(corr, np.array([0, 1]))
    first_raw = corr[72:]
    scale_factor = lax.rsqrt(jnp.sum(first_raw * first_raw) * (1.0 / 128.0) + 1e-06)
    correlator = jnp.stack([corr[:64, :64], corr[:64, 64:]])[None]
    raw = jnp.stack([corr[64:72, :8], corr[64:72, 8:16]])
    return (correlator, (raw * scale_factor)[None])


def solution(mesh):
    placed = (
        P("ta", "gx", None, None, None),
        P("ta", None, "gx", None, None, None),
        P(),
        P(),
        P(),
        P(),
        P(),
    )
    return jax.shard_map(
        body,
        mesh=mesh,
        in_specs=placed,
        out_specs=(P("ta", None, None, None), P("ta", None, None, None)),
        check_vma=False,
    )
```

```python
import functools
import math

import jax
import jax.numpy as jnp
import numpy as np
from jax import lax
from jax.experimental import pallas as pl
from jax.experimental.pallas import tpu as pltpu
from jax.sharding import PartitionSpec as P

EXTENT = 96
NMOM = 9
BF = jnp.bfloat16
F32 = jnp.float32
HALF_PERIOD = -2.0 * math.pi / EXTENT
CHUNK = 768
ROWS = 24
MPAD = 16
VMEM = 60 << 20
full_precision = lax.Precision.HIGHEST
SAME_CORE = [[d for d in range(32) if d % 2 == c] for c in range(2)]
PAIR = [(d, d ^ 1) for d in range(32)]


def shift(x, z):
    ring = [(i, j, c) for i in range(4) for j in range(4) for c in range(2)]
    number = lambda i, j, c: i % 4 * 8 + j % 4 * 2 + c
    return [(number(i, j, c), number(i + x, j + z, c)) for i, j, c in ring]


def gamma_tables():
    zero_block = np.zeros((4, 4), np.float32)
    first_imag = np.array([[0, 0, 0, 1], [0, 0, 1, 0], [0, -1, 0, 0], [-1, 0, 0, 0]], np.float32)
    second_real = np.array([[0, 0, 0, -1], [0, 0, 1, 0], [0, 1, 0, 0], [-1, 0, 0, 0]], np.float32)
    third_imag = np.array([[0, 0, 1, 0], [0, 0, 0, -1], [-1, 0, 0, 0], [0, 1, 0, 0]], np.float32)
    fourth_real = np.array([[0, 0, 1, 0], [0, 0, 0, 1], [1, 0, 0, 0], [0, 1, 0, 0]], np.float32)
    gamma_list = [
        (zero_block, first_imag),
        (second_real, zero_block),
        (zero_block, third_imag),
        (fourth_real, zero_block),
    ]
    real_parts = []
    imag_parts = []
    for subset in range(16):
        prod_real = np.eye(4, dtype=np.float32)
        prod_imag = np.zeros((4, 4), np.float32)
        for position in range(4):
            if subset >> position & 1:
                factor_real, factor_imag = gamma_list[position]
                prod_real, prod_imag = (
                    prod_real @ factor_real - prod_imag @ factor_imag,
                    prod_real @ factor_imag + prod_imag @ factor_real,
                )
        real_parts.append(prod_real)
        imag_parts.append(prod_imag)
    return (np.stack(real_parts).astype(np.float32), np.stack(imag_parts).astype(np.float32))


def spin_tables():
    chiral = np.array([1.0, 1.0, -1.0, -1.0], np.float32)
    parts = np.stack(gamma_tables())
    left = np.transpose(parts, (0, 2, 1, 3)) * chiral[None, :, None, None]
    left = np.repeat(left[..., None], MPAD, -1).reshape(2, 4, 16, 4 * MPAD)
    right = np.transpose(parts, (0, 3, 1, 2)) * chiral
    right = right * np.array([1.0, -1.0], np.float32)[:, None, None, None]
    right = np.broadcast_to(right[:, :, :, None, None, :], (2, 4, 16, NMOM, 4, 4))
    return left, right.reshape(2, 4, 16, NMOM * 16)


def dot(left, right, lc, rc, precision=None):
    return lax.dot_general(
        left, right, (((lc,), (rc,)), ((), ())), precision=precision, preferred_element_type=F32
    )


def phase_kernel(first, full, half, steps, where_ref, mom_ref, own_ref, other_ref, out_ref, acc_ref):
    step = pl.program_id(0)
    core = lax.rem(where_ref[0], 2)
    is_own = step < steps
    real = jnp.where(is_own, own_ref[0], other_ref[0])
    imag = jnp.where(is_own, own_ref[1], other_ref[1])
    left = jnp.concatenate([real.T, imag.T], 1)
    device = jnp.where(is_own, where_ref[0], where_ref[0] + 1 - 2 * core)
    unit = lax.broadcasted_iota(jnp.int32, (8, CHUNK), 0)
    row = lax.rem(step, steps) * CHUNK + lax.broadcasted_iota(jnp.int32, (8, CHUNK), 1)
    site = jnp.floor((row.astype(F32) + 0.5) * (1.0 / 3.0)) + (device * 512).astype(F32)
    line = jnp.floor((site + 0.5) * (1.0 / EXTENT))
    xcoord = site - EXTENT * line
    zcoord = jnp.floor((line + 0.5) * (1.0 / EXTENT))
    ycoord = line - EXTENT * zcoord
    winding = jnp.zeros((8, CHUNK), F32)
    for u in range(full + half):
        m = 4 * core + first + u if u < full else NMOM - 1
        here = (
            mom_ref[3 * m].astype(F32) * xcoord
            + mom_ref[3 * m + 1].astype(F32) * ycoord
            + mom_ref[3 * m + 2].astype(F32) * zcoord
        )
        winding = jnp.where(unit == u, here, winding)
    winding = winding - EXTENT * jnp.floor((winding + 0.5) * (1.0 / EXTENT))
    angle = winding * HALF_PERIOD
    cosine = jnp.cos(angle)
    sine = jnp.sin(angle)
    if half:
        turned = jnp.logical_and(unit == full, core == 1)
        cosine, sine = jnp.where(turned, sine, cosine), jnp.where(turned, -cosine, sine)
    cosine = cosine.T
    sine = sine.T
    real = real.astype(F32)
    imag = imag.astype(F32)

    @pl.when(step == 0)
    def _():
        acc_ref[...] = jnp.zeros_like(acc_ref)

    for u in range(full + half):
        c = cosine[:, u : u + 1]
        s = sine[:, u : u + 1]
        twist_real = (c * real - s * imag).astype(BF)
        twist_imag = (c * imag + s * real).astype(BF)
        if u < full:
            right = jnp.concatenate(
                [
                    jnp.concatenate([twist_real, twist_imag], 1),
                    jnp.concatenate([twist_imag, -twist_real], 1),
                ],
                0,
            )
        else:
            right = jnp.concatenate([twist_real, twist_imag], 0)
        at = slice(768 * u, 768 * u + right.shape[1])
        acc_ref[:, at] += dot(left, right, 1, 0)

    @pl.when(step == 2 * steps - 1)
    def _():
        width = acc_ref.shape[1]
        diagonal = lax.broadcasted_iota(jnp.int32, (384, 384), 0) == lax.broadcasted_iota(
            jnp.int32, (384, 384), 1
        )
        lane = lax.broadcasted_iota(jnp.int32, (384, 128), 1)
        rest = jnp.zeros((384, 128), F32)
        for b in range(width // 384):
            block = acc_ref[:, 384 * b : 384 * b + 384]
            lost = jnp.where(diagonal, block - block.astype(BF).astype(F32), 0.0)
            rest = jnp.where(lane == b, jnp.sum(lost, 1, keepdims=True), rest)
        for j in range(16):
            at = slice(ROWS * j, ROWS * (j + 1))
            out_ref[j, :, :width] = acc_ref[at, :].astype(BF)
            out_ref[j, :, width:] = rest[at].astype(BF)


def phase_part(own, other, where, momenta, first, full, half):
    steps = own.shape[1] // CHUNK
    width = 768 * full + 384 * half
    return pl.pallas_call(
        functools.partial(phase_kernel, first, full, half, steps),
        grid_spec=pltpu.PrefetchScalarGridSpec(
            num_scalar_prefetch=2,
            grid=(2 * steps,),
            in_specs=[
                pl.BlockSpec((2, CHUNK, 384), lambda c, *_: (0, jnp.minimum(c, steps - 1), 0)),
                pl.BlockSpec((2, CHUNK, 384), lambda c, *_: (0, jnp.maximum(c - steps, 0), 0)),
            ],
            out_specs=pl.BlockSpec((16, ROWS, width + 128), lambda c, *_: (0, 0, 0)),
            scratch_shapes=[pltpu.VMEM((384, width), F32)],
        ),
        out_shape=jax.ShapeDtypeStruct((16, ROWS, width + 128), BF),
        compiler_params=pltpu.CompilerParams(vmem_limit_bytes=VMEM),
        cost_estimate=pl.CostEstimate(
            flops=4 * 384 * 6144 * width, transcendentals=0, bytes_accessed=6 << 20
        ),
        name=f"phase_{first}",
    )(where, momenta, own, other)


def source_kernel(
    where_ref, tau_ref, src_ref, mom_ref, gam_ref, ltab_ref, rtab_ref, vec_ref,
    out_ref, left_ref, right_ref, basis_ref,
):
    n = pl.program_id(0)
    x = jnp.concatenate([tau_ref[:, 0].reshape(384, 384), tau_ref[:, 1].reshape(384, 384)], 1)
    s_real = src_ref[0, 0]
    s_imag = src_ref[0, 1]
    to_real = jnp.concatenate([s_real, s_imag], 1)
    to_imag = jnp.concatenate([s_imag, -s_real], 1)
    out_ref[:, 0, 0] = dot(x, to_real, 1, 1).astype(BF).reshape(ROWS, 16, 192)
    out_ref[:, 1, 0] = dot(x, to_imag, 1, 1).astype(BF).reshape(ROWS, 16, 192)

    @pl.when(n == 0)
    def _():
        basis_ref[...] = vec_ref[...]
        chosen = (gam_ref[...] == lax.broadcasted_iota(jnp.int32, (64, 16), 1)).astype(BF)
        lane = lax.rem(lax.broadcasted_iota(jnp.int32, (64, 64), 1), MPAD)
        moment = mom_ref[...] == lane
        for a in range(4):
            for q in range(2):
                got = jnp.where(moment, dot(chosen, ltab_ref[q, a], 1, 0), 0.0)
                left_ref[q, 64 * a : 64 * a + 64, :] = got
        lane = lax.broadcasted_iota(jnp.int32, (64, 144), 1)
        low = mom_ref[...] * 16
        moment = jnp.logical_and(lane >= low, lane < low + 16)
        for y in range(4):
            for q in range(2):
                right_ref[q, y] = jnp.where(moment, dot(chosen, rtab_ref[q, y], 1, 0), 0.0)


def source_part(tau, source_blocks, op_momentum, op_gamma, ref_vectors, where):
    ltab, rtab = spin_tables()
    whole = lambda shape: pl.BlockSpec(shape, lambda n, *_: (0,) * len(shape))
    return pl.pallas_call(
        source_kernel,
        grid_spec=pltpu.PrefetchScalarGridSpec(
            num_scalar_prefetch=1,
            grid=(NMOM,),
            in_specs=[
                whole((ROWS, 2, 16, 384)),
                pl.BlockSpec((1, 2, 192, 384), lambda n, w: (n, 0, lax.rem(w[0], 2), 0)),
                whole((64, 1)),
                whole((64, 1)),
                whole((2, 4, 16, 64)),
                whole((2, 4, 16, 144)),
                whole((2, 64, 8)),
            ],
            out_specs=[
                pl.BlockSpec((ROWS, 2, 1, 16, 192), lambda n, *_: (0, 0, n, 0, 0)),
                whole((2, 256, 64)),
                whole((2, 4, 64, 144)),
                whole((2, 64, 8)),
            ],
        ),
        out_shape=[
            jax.ShapeDtypeStruct((ROWS, 2, NMOM, 16, 192), BF),
            jax.ShapeDtypeStruct((2, 256, 64), F32),
            jax.ShapeDtypeStruct((2, 4, 64, 144), F32),
            jax.ShapeDtypeStruct((2, 64, 8), F32),
        ],
        compiler_params=pltpu.CompilerParams(vmem_limit_bytes=VMEM),
        cost_estimate=pl.CostEstimate(
            flops=8 * 384 * 384 * 1728, transcendentals=0, bytes_accessed=8 << 20
        ),
        name="source",
    )(
        where,
        tau,
        source_blocks,
        op_momentum[:, None],
        op_gamma[:, None],
        jnp.asarray(ltab, BF),
        jnp.asarray(rtab, BF),
        ref_vectors,
    )


def thirds(value):
    high = value.astype(BF)
    rest = value - high.astype(F32)
    middle = rest.astype(BF)
    return [high, middle, (rest - middle.astype(F32)).astype(BF)]


def sink_kernel(
    where_ref, own1, oth1, own2, oth2, tau_hbm, src_hbm, left_ref, right_ref, basis_ref, out_ref,
    rows_ref, sink_ref, acc_ref, tau_ref, src_ref, sem,
):
    core = lax.rem(where_ref[0], 2)
    fetches = []
    for g in range(4):
        for q in range(2):
            source = tau_hbm.at[:, pl.ds(3072 * q + 768 * g, 768)]
            target = tau_ref.at[q, :, pl.ds(768 * g, 768)]
            fetches.append(pltpu.make_async_copy(source, target, sem.at[2 * g + q]))
    fetches.append(pltpu.make_async_copy(src_hbm, src_ref, sem.at[8]))
    for fetch in fetches:
        fetch.start()
    rows_ref[...] = jnp.zeros_like(rows_ref)
    for c in range(2):
        one = jnp.where(core == c, own1[...], oth1[...]).astype(F32)
        two = jnp.where(core == c, own2[...], oth2[...]).astype(F32)
        for u in range(4):
            part = one if u < 1 else two
            for q in range(2):
                at = 768 * max(u - 1, 0) + 384 * q
                rows_ref[q, :, 4 * c + u, :] = part[:, at : at + 384]
        rows_ref[c, :, 8, :] = one[:, 768:1152]
    real = rows_ref[0].reshape(384, 384).astype(BF)
    imag = rows_ref[1].reshape(384, 384).astype(BF)
    stacked = jnp.concatenate(
        [jnp.concatenate([real, -imag], 1), jnp.concatenate([imag, real], 1)], 0
    )
    for g in range(4):
        fetches[2 * g].wait()
        fetches[2 * g + 1].wait()
        at = slice(768 * g, 768 * g + 768)
        here = jnp.concatenate([tau_ref[0, :, at], tau_ref[1, :, at]], 0)
        got = dot(stacked, here, 1, 0).astype(BF)
        for y in range(4):
            for q in range(2):
                sink_ref[q, 4 * y + g] = got[384 * q : 384 * q + 384, 192 * y : 192 * y + 192]
    acc_ref[...] = jnp.zeros_like(acc_ref)
    fetches[8].wait()

    def one_row(r, carry):
        at = pl.ds(pl.multiple_of(r * MPAD, MPAD), MPAD)
        left = jnp.concatenate([sink_ref[q, :, at, :].reshape(256, 192) for q in range(2)], 0)
        right = src_ref[r].reshape(288, 192)
        acc_ref[...] += dot(right, left, 1, 1)
        return carry

    lax.fori_loop(0, ROWS, one_row, 0, unroll=12)
    acc = acc_ref[...]
    block_real = acc[:144, :256] - acc[144:, 256:]
    block_imag = acc[144:, :256] + acc[:144, 256:]
    l_real = left_ref[0]
    l_imag = left_ref[1]
    lifted = jnp.concatenate(
        [jnp.concatenate([l_real, -l_imag], 1), jnp.concatenate([l_imag, l_real], 1)], 0
    ).astype(BF)
    lifted = jnp.concatenate([lifted] * 3, 1)
    spin = lax.rem(lax.broadcasted_iota(jnp.int32, (64, 144), 1), 16) // 4
    corr_real = jnp.zeros((64, 64), F32)
    corr_imag = jnp.zeros((64, 64), F32)
    for y in range(4):
        at = slice(64 * y, 64 * y + 64)
        both = thirds(jnp.concatenate([block_real[:, at], block_imag[:, at]], 1))
        got = dot(lifted, jnp.concatenate(both, 1), 1, 1)
        halves = []
        for q in range(2):
            total = jnp.zeros((64, 144), F32)
            for a in range(4):
                low = 256 * q + 64 * a
                total = jnp.where(spin == a, got[low : low + 64], total)
            halves.append(total)
        r_real = right_ref[0, y]
        r_imag = right_ref[1, y]
        weights = jnp.concatenate([r_real, r_imag], 0).astype(BF)
        lhs = jnp.concatenate(thirds(jnp.concatenate(halves, 0)), 0)
        got = dot(lhs, weights, 1, 1)
        got = got[:128] + got[128:256] + got[256:]
        corr_real += got[:64, :64] - got[64:, 64:]
        corr_imag += got[:64, 64:] + got[64:, :64]
    b_real = basis_ref[0]
    b_imag = basis_ref[1]
    exact = functools.partial(dot, precision=full_precision)
    half_real = exact(corr_real, b_real, 1, 0) - exact(corr_imag, b_imag, 1, 0)
    half_imag = exact(corr_real, b_imag, 1, 0) + exact(corr_imag, b_real, 1, 0)
    out_ref[:64, :64] = corr_real
    out_ref[:64, 64:] = corr_imag
    out_ref[64:, :] = jnp.zeros((8, 128), F32)
    out_ref[64:, :8] = exact(b_real, half_real, 0, 0) + exact(b_imag, half_imag, 0, 0)
    out_ref[64:, 8:16] = exact(b_real, half_imag, 0, 0) - exact(b_imag, half_real, 0, 0)


def sink_part(where, own1, oth1, own2, oth2, tau, src, left, right, basis):
    inside = pl.BlockSpec(memory_space=pltpu.VMEM)
    outside = pl.BlockSpec(memory_space=pl.ANY)
    specs = [inside] * 4 + [outside] * 2 + [inside] * 3
    return pl.pallas_call(
        sink_kernel,
        grid_spec=pltpu.PrefetchScalarGridSpec(
            num_scalar_prefetch=1,
            grid=(),
            in_specs=specs,
            out_specs=pl.BlockSpec(memory_space=pltpu.VMEM),
            scratch_shapes=[
                pltpu.VMEM((2, ROWS, MPAD, 384), F32),
                pltpu.VMEM((2, 16, 384, 192), BF),
                pltpu.VMEM((288, 512), F32),
                pltpu.VMEM((2, 384, 3072), BF),
                pltpu.VMEM((ROWS, 2, NMOM, 16, 192), BF),
                pltpu.SemaphoreType.DMA((9,)),
            ],
        ),
        out_shape=jax.ShapeDtypeStruct((72, 128), F32),
        compiler_params=pltpu.CompilerParams(vmem_limit_bytes=VMEM),
        name="sink",
    )(where, own1, oth1, own2, oth2, tau, src, left, right, basis)


def around(shard, axis):
    sent = [lax.ppermute(shard, "gx", shift(*(axis * d))) for d in (1, 3, 2)]
    return shard + sent[0] + sent[1] + sent[2]


def exchanged(part):
    return lax.all_to_all(part, "gx", 0, 0, tiled=True, axis_index_groups=SAME_CORE)


def summed(got, chip):
    total = jnp.sum(got.astype(F32), 0)
    width = total.shape[1] - 128
    lane = lax.broadcasted_iota(jnp.int32, (ROWS, width), 1)
    row = lax.broadcasted_iota(jnp.int32, (ROWS, width), 0)
    rest = jnp.zeros((ROWS, width), F32)
    for b in range(width // 384):
        diagonal = lane == 384 * b + ROWS * chip + row
        rest = jnp.where(diagonal, total[:, width + b : width + b + 1], rest)
    return (total[:, :width] + rest).astype(BF)


def body(eigvecs, perambulators, source_blocks, momenta, op_momentum, op_gamma, ref_vectors):
    device = lax.axis_index("gx")
    core = device % 2
    where = device[None]
    mixed = eigvecs.reshape(-1, 2, 384)
    own = jnp.transpose(mixed, (1, 0, 2))
    other = jnp.transpose(lax.ppermute(mixed, "gx", PAIR), (1, 0, 2))
    own, perambulators = lax.optimization_barrier((own, perambulators))
    mine = jnp.transpose(perambulators[0], (1, 0, 2, 3, 4)).reshape(12, 2, 16, 384)
    theirs = lax.ppermute(mine, "gx", PAIR)
    tau = jnp.where(
        core == 0, jnp.concatenate([mine, theirs], 0), jnp.concatenate([theirs, mine], 0)
    )
    part = jnp.where(core == 0, tau[..., :192], tau[..., 192:]).reshape(ROWS, 6144)
    tau_all = lax.all_gather(part, "gx", axis=0, tiled=True, axis_index_groups=SAME_CORE)
    flat = momenta.reshape(-1)
    first = phase_part(own, other, where, flat, 0, 1, 1)
    own, first = lax.optimization_barrier((own, first))
    got1 = exchanged(first)
    second = phase_part(own, other, where, flat, 1, 3, 0)
    tau, second = lax.optimization_barrier((tau, second))
    got2 = exchanged(second)
    src, left, right, basis = source_part(
        tau, source_blocks, op_momentum, op_gamma, ref_vectors, where
    )
    own1 = summed(got1, device // 2)
    oth1 = lax.ppermute(own1, "gx", PAIR)
    got2, src, oth1 = lax.optimization_barrier((got2, src, oth1))
    own2 = summed(got2, device // 2)
    oth2 = lax.ppermute(own2, "gx", PAIR)
    corr = sink_part(where, own1, oth1, own2, oth2, tau_all, src, left, right, basis)
    corr = corr + lax.ppermute(corr, "gx", PAIR)
    raw = corr[64:]
    first_raw = jnp.where(lax.axis_index("ta") == 0, raw, 0.0)
    for t in (1, 3, 2):
        first_raw = first_raw + lax.ppermute(raw, "ta", [(0, t)])
    corr = jnp.concatenate([corr, first_raw], 0)
    corr = around(corr, np.array([1, 0]))
    corr = around(corr, np.array([0, 1]))
    first_raw = corr[72:]
    scale_factor = lax.rsqrt(jnp.sum(first_raw * first_raw) * (1.0 / 128.0) + 1e-06)
    correlator = jnp.stack([corr[:64, :64], corr[:64, 64:]])[None]
    raw = jnp.stack([corr[64:72, :8], corr[64:72, 8:16]])
    return (correlator, (raw * scale_factor)[None])


def solution(mesh):
    placed = (
        P("ta", "gx", None, None, None),
        P("ta", None, "gx", None, None, None),
        P(),
        P(),
        P(),
        P(),
        P(),
    )
    return jax.shard_map(
        body,
        mesh=mesh,
        in_specs=placed,
        out_specs=(P("ta", None, None, None), P("ta", None, None, None)),
        check_vma=False,
    )
```
